32 devices in a mesh: section: 2 (over core), seq: 16 (over z, y, x).
Axes of the slice: x: 2, y: 2, z: 4, core: 2. Of those that a mesh axis runs over, the one named last changes fastest.
Arguments:
- queries: bfloat16 [4096, 4096], P('seq', 'section'), may hold values from -50 to 50
- key_rows: bfloat16 [4096, 4096], P('seq', 'section'), may hold values from -6 to 6
- value_rows: bfloat16 [4096, 4096], P('seq', 'section'), may hold values from -6 to 6
- block_pattern: int32 [32, 8], P('seq'), may hold values from 0 to 1, as said below
- out_weight: bfloat16 [4096, 4096], P('section'), may hold values from -0.09375 to 0.09375
- hidden: bfloat16 [4096, 4096], P('seq', 'section'), may hold values from -3 to 3
- norm_gain: float32 [4096], P('section'), may hold values from 0.5 to 1.5
Outputs:
- stream_out: bfloat16 [4096, 4096], P('seq', 'section')
- normed: bfloat16 [4096, 4096], P('seq', 'section')
The draws below stay inside these ranges and needn't reach their ends.
Inputs may be any that keep to these rules, and one draw needn't show every extreme that they name: `block_pattern`: column 0 is 1 in every row: every query block attends its own block.
All inputs are finite; a program needn't handle non-finite values.
Results may differ from the reference program's by a relative error of at most 0.008.
Values may be sent and summed in bfloat16 or wider, within the bound.
A program may use at most 128 MiB of HBM per device.

```python
import math
import jax
import jax.numpy as jnp
from jax import lax

D = 4096
HEADS = 32
HEAD_DIM = 128
BLOCK = 128
WINDOW_BLOCKS = 8
TOKENS = 4096
NBLK = 32
N_SECTION = 2


def joint_draw(key):
    full_shape = (TOKENS, D)
    query_key = jax.random.fold_in(key, 101)
    keys_key = jax.random.fold_in(key, 202)
    query_draw = jnp.clip(2.0 * jax.random.normal(query_key, full_shape, jnp.float32), -12.0, 12.0)
    key_draw = jnp.clip(jax.random.normal(keys_key, full_shape, jnp.float32), -6.0, 6.0)
    return (query_draw, key_draw)


def draw_queries(key, part):
    query_draw, key_draw = joint_draw(key)
    return query_draw.astype(jnp.bfloat16)


def draw_key_rows(key, part):
    query_draw, key_draw = joint_draw(key)
    return key_draw.astype(jnp.bfloat16)


def draw_block_pattern(key, part):
    picked = jax.random.randint(jax.random.fold_in(key, 303), (NBLK, WINDOW_BLOCKS), 0, 2, jnp.int32)
    column = jnp.arange(WINDOW_BLOCKS, dtype=jnp.int32)[None, :]
    return jnp.where(column == 0, 1, picked).astype(jnp.int32)


def draw_hidden(key, part):
    column_scale = 0.5 + jnp.arange(D, dtype=jnp.float32) / D
    base_key = jax.random.fold_in(key, 404)
    noise = jnp.clip(jax.random.normal(base_key, (TOKENS, D), jnp.float32), -6.0, 6.0)
    values = 0.3 * noise * column_scale[None, :]
    return values.astype(jnp.bfloat16)


def block_levels(rng, extent, shards, low, top_value):
    def one(dim, blocks):
        draws = jax.random.uniform(jax.random.fold_in(jax.random.fold_in(rng, 6), dim), (blocks,), jnp.float32, low / len(shards), top_value / len(shards))
        return jnp.repeat(jnp.exp(draws), extent[dim] // blocks).reshape((-1,) + (1,) * (len(extent) - dim - 1))

    level = one(*shards[0])
    for cut in shards[1:]:
        level = level * one(*cut)
    return level


def gaussian(key, dims, deviation, bound, pieces=(), kind=jnp.bfloat16):
    values = deviation * jax.random.normal(key, dims, jnp.float32)
    if pieces:
        values = values * block_levels(key, dims, pieces, -0.22, 0.18)
    return jnp.clip(values, -bound, bound).astype(kind)


def setup_inputs(seed: int = 0) -> dict:
    keys = jax.random.split(jax.random.key(seed), 8)
    return {
        "queries": draw_queries(jax.random.fold_in(keys[7], 71), 0),
        "key_rows": draw_key_rows(jax.random.fold_in(keys[7], 71), 0),
        "value_rows": gaussian(keys[2], (TOKENS, D), 1.0, 6.0, ((0, 16), (1, 2))),
        "block_pattern": draw_block_pattern(jax.random.fold_in(keys[7], 71), 0),
        "out_weight": gaussian(keys[4], (D, D), D ** -0.5, 0.09375, ((0, 2),)),
        "hidden": draw_hidden(jax.random.fold_in(keys[7], 71), 0),
        "norm_gain": jnp.clip(1.0 + 0.1 * jax.random.normal(keys[6], (D,), jnp.float32), 0.5, 1.5),
    }


def window_attention(queries, key_rows, value_rows, block_pattern):
    token_count = queries.shape[0]
    block_count = token_count // BLOCK
    front_rows = (WINDOW_BLOCKS - 1) * BLOCK
    padded_keys = jnp.concatenate([jnp.zeros((front_rows, D), key_rows.dtype), key_rows], 0)
    padded_values = jnp.concatenate([jnp.zeros((front_rows, D), value_rows.dtype), value_rows], 0)
    window_span = WINDOW_BLOCKS * BLOCK
    offsets = (WINDOW_BLOCKS - 1 - jnp.arange(window_span, dtype=jnp.int32) // BLOCK).astype(jnp.int32)
    key_place = jnp.arange(window_span, dtype=jnp.int32) % BLOCK
    query_place = jnp.arange(BLOCK, dtype=jnp.int32)
    scaling = 1.0 / math.sqrt(HEAD_DIM)

    def one_block(block_index):
        begin_row = (block_index * BLOCK).astype(jnp.int32)
        query_block = lax.dynamic_slice_in_dim(queries, begin_row, BLOCK, 0).astype(jnp.float32).reshape(BLOCK, HEADS, HEAD_DIM)
        key_block = lax.dynamic_slice_in_dim(padded_keys, begin_row, window_span, 0).astype(jnp.float32).reshape(window_span, HEADS, HEAD_DIM)
        value_block = lax.dynamic_slice_in_dim(padded_values, begin_row, window_span, 0).astype(jnp.float32).reshape(window_span, HEADS, HEAD_DIM)
        pattern_row = lax.dynamic_index_in_dim(block_pattern, block_index, 0, keepdims=False)
        allowed = (pattern_row[offsets] == 1) & (block_index - offsets >= 0)
        causal = (offsets[None, :] > 0) | (key_place[None, :] <= query_place[:, None])
        visible = allowed[None, :] & causal
        scores = jnp.einsum('qhd,khd->hqk', query_block, key_block) * scaling
        scores = jnp.where(visible[None], scores, -jnp.inf)
        largest = lax.optimization_barrier(jnp.max(scores, axis=2, keepdims=True))
        exponent = jnp.exp(scores - largest)
        weights = (exponent / lax.optimization_barrier(jnp.sum(exponent, axis=2, keepdims=True))).astype(jnp.bfloat16)
        mixture = jnp.einsum('hqk,khd->qhd', weights.astype(jnp.float32), value_block)
        return mixture.reshape(BLOCK, D).astype(jnp.bfloat16)
    result = lax.map(one_block, jnp.arange(block_count, dtype=jnp.int32))
    return result.reshape(token_count, D)

def reference(queries, key_rows, value_rows, block_pattern, out_weight, hidden, norm_gain):
    attended = window_attention(queries, key_rows, value_rows, block_pattern)
    group_width = D // N_SECTION
    projected = jnp.zeros((TOKENS, D), jnp.float32)
    for group_index in range(N_SECTION):
        low = group_index * group_width
        group_part = jnp.dot(attended[:, low:low + group_width], out_weight[low:low + group_width], preferred_element_type=jnp.float32).astype(jnp.bfloat16)
        projected = projected + lax.optimization_barrier(group_part).astype(jnp.float32)
    stream = hidden.astype(jnp.float32) + projected
    mean_square = lax.optimization_barrier(jnp.mean(stream * stream, axis=1, keepdims=True))
    normed = stream * lax.rsqrt(mean_square + 1e-06) * norm_gain[None, :]
    return (stream.astype(jnp.bfloat16), normed.astype(jnp.bfloat16))
```

```python
import math

import jax
import jax.numpy as jnp
from jax import lax
from jax.experimental import pallas as pl
from jax.experimental.pallas import tpu as pltpu
from jax.sharding import PartitionSpec as P

HEAD_DIM = 128
BLOCK = 128
WINDOW_BLOCKS = 8
GROUP = 4
MESH = pl.DeviceIdType.MESH
HIDE = -1e30


def kernel(
    q_hbm, k_hbm, v_hbm, pattern_hbm, w_hbm, h_hbm,
    stream_ref, square_ref,
    kv, qbuf, obuf, amix, wbuf, hbuf, patterns, bias, acc,
    mine, outgoing, incoming, square_out, square_in,
    kv_own, q_own, pat_own, w_sem, h_sem,
    kv_send, kv_recv, z_send, q_send, q_recv, o_send, o_recv, pat_send, pat_recv,
    part_send, part_recv, sq_sem,
):
    rows, width = q_hbm.shape
    model = w_hbm.shape[1]
    heads = kv.shape[1]
    blocks = rows // BLOCK
    front = (WINDOW_BLOCKS - 1) * BLOCK
    span = front + rows
    skip = GROUP * rows - front
    shard = lax.axis_index("seq")
    section = lax.axis_index("section")
    count = lax.axis_size("seq")
    role = lax.rem(shard, GROUP)
    first_shard = shard - role
    has_prev = shard >= GROUP
    has_next = shard + GROUP < count
    partner = 1 - section
    low = lax.rem(role, 2)
    high = role // 2
    peers = (3 - role, 2 * high + 1 - low, 2 * (1 - high) + low)
    sources = (k_hbm, v_hbm)

    def head_cols(home, n):
        return pl.ds(pl.multiple_of((home * heads + n) * HEAD_DIM, HEAD_DIM), HEAD_DIM)

    def place(slot):
        return pl.ds(pl.multiple_of(slot * rows, rows), rows)

    def to_peer(peer):
        return {"seq": first_shard + peer}

    def kv_local(i, n):
        return pltpu.make_async_copy(
            sources[i].at[:, head_cols(role, n)],
            kv.at[i, n, place(GROUP + role), :],
            kv_own.at[i, n],
        )

    def q_local(n):
        return pltpu.make_async_copy(
            q_hbm.at[:, head_cols(role, n)], qbuf.at[n, place(role), :], q_own.at[n]
        )

    def kv_copy(i, n, e):
        return pltpu.make_async_remote_copy(
            src_ref=sources[i].at[:, head_cols(peers[e], n)],
            dst_ref=kv.at[i, n, place(GROUP + role), :],
            send_sem=kv_send.at[i, n, e],
            recv_sem=kv_recv.at[i, n, GROUP + role],
            device_id=to_peer(peers[e]),
            device_id_type=MESH,
        )

    def kv_arrive(i, n, slot):
        pltpu.make_async_remote_copy(
            src_ref=kv.at[i, n, place(slot), :],
            dst_ref=kv.at[i, n, place(slot), :],
            send_sem=kv_send.at[i, n, 0],
            recv_sem=kv_recv.at[i, n, slot],
            device_id={"section": partner},
            device_id_type=MESH,
        ).wait_recv()

    def q_copy(n, e):
        return pltpu.make_async_remote_copy(
            src_ref=q_hbm.at[:, head_cols(peers[e], n)],
            dst_ref=qbuf.at[n, place(role), :],
            send_sem=q_send.at[n, e],
            recv_sem=q_recv.at[n, role],
            device_id=to_peer(peers[e]),
            device_id_type=MESH,
        )

    def q_arrive(n, c):
        pltpu.make_async_remote_copy(
            src_ref=qbuf.at[n, place(c), :],
            dst_ref=qbuf.at[n, place(c), :],
            send_sem=q_send.at[n, 0],
            recv_sem=q_recv.at[n, c],
            device_id={"section": partner},
            device_id_type=MESH,
        ).wait_recv()

    def mix_cols(c):
        return pl.ds(pl.multiple_of(c * HEAD_DIM, HEAD_DIM), HEAD_DIM)

    def o_copy(n, c):
        return pltpu.make_async_remote_copy(
            src_ref=obuf.at[n, place(c), :],
            dst_ref=amix.at[n, :, mix_cols(role)],
            send_sem=o_send.at[n, c],
            recv_sem=o_recv.at[n, role],
            device_id=to_peer(c),
            device_id_type=MESH,
        )

    def o_arrive(n, c):
        pltpu.make_async_remote_copy(
            src_ref=amix.at[n, :, mix_cols(c)],
            dst_ref=amix.at[n, :, mix_cols(c)],
            send_sem=o_send.at[n, 0],
            recv_sem=o_recv.at[n, c],
            device_id={"section": partner},
            device_id_type=MESH,
        ).wait_recv()

    def pat_copy(e):
        return pltpu.make_async_remote_copy(
            src_ref=pattern_hbm,
            dst_ref=patterns.at[role],
            send_sem=pat_send.at[e],
            recv_sem=pat_recv.at[role],
            device_id=to_peer(peers[e]),
            device_id_type=MESH,
        )

    def pat_arrive(c):
        pltpu.make_async_remote_copy(
            src_ref=patterns.at[c],
            dst_ref=patterns.at[c],
            send_sem=pat_send.at[0],
            recv_sem=pat_recv.at[c],
            device_id={"section": partner},
            device_id_type=MESH,
        ).wait_recv()

    def z_copies(i, n, c, own):
        def one(first, extent):
            if own:
                source = sources[i].at[pl.ds(first, extent), head_cols(role, n)]
            else:
                source = kv.at[
                    i, n, pl.ds(pl.multiple_of((GROUP + c) * rows + first, BLOCK), extent), :
                ]
            return pltpu.make_async_remote_copy(
                src_ref=source,
                dst_ref=kv.at[i, n, pl.ds(pl.multiple_of(c * rows + first, BLOCK), extent), :],
                send_sem=z_send.at[i, n, c],
                recv_sem=kv_recv.at[i, n, c],
                device_id={"seq": shard + GROUP},
                device_id_type=MESH,
            )

        return one(skip, rows - skip), one(0, rows)

    def z_act(i, n, c, own, act):
        tail, full = z_copies(i, n, c, own)

        @pl.when(has_next & (c == 0))
        def _():
            act(tail)

        @pl.when(has_next & (c > 0))
        def _():
            act(full)

    def z_start(i, n, c, own):
        z_act(i, n, c, own, lambda copy: copy.start())

    def z_end(i, n, c):
        z_act(i, n, c, False, lambda copy: copy.wait_send())

    def z_arrive(n, c):
        @pl.when(has_prev)
        def _():
            for i in range(2):
                tail = pl.ds(c * rows + (skip if c == 0 else 0), rows - (skip if c == 0 else 0))
                pltpu.make_async_remote_copy(
                    src_ref=kv.at[i, n, tail, :],
                    dst_ref=kv.at[i, n, tail, :],
                    send_sem=z_send.at[i, n, 0],
                    recv_sem=kv_recv.at[i, n, c],
                    device_id={"section": partner},
                    device_id_type=MESH,
                ).wait_recv()

    def w_copy(n, c):
        return pltpu.make_async_copy(
            w_hbm.at[pl.ds((c * heads + n) * HEAD_DIM, HEAD_DIM), :],
            wbuf.at[pl.ds((n * GROUP + c) * HEAD_DIM, HEAD_DIM), :],
            w_sem.at[n, c],
        )

    h_load = pltpu.make_async_copy(h_hbm, hbuf, h_sem.at[0])
    pat_load = pltpu.make_async_copy(pattern_hbm, patterns.at[role], pat_own.at[0])

    barrier = pltpu.get_barrier_semaphore()
    for e in range(GROUP - 1):
        pl.semaphore_signal(barrier, inc=1, device_id=to_peer(peers[e]), device_id_type=MESH)
    pl.semaphore_signal(barrier, inc=1, device_id={"section": partner}, device_id_type=MESH)

    @pl.when(has_prev)
    def _():
        pl.semaphore_signal(
            barrier, inc=1, device_id={"seq": shard - GROUP}, device_id_type=MESH
        )

    @pl.when(has_next)
    def _():
        pl.semaphore_signal(
            barrier, inc=1, device_id={"seq": shard + GROUP}, device_id_type=MESH
        )

    pat_load.start()
    for n in range(heads):
        for i in range(2):
            kv_local(i, n).start()
        q_local(n).start()

    pl.semaphore_wait(
        barrier, GROUP + has_prev.astype(jnp.int32) + has_next.astype(jnp.int32)
    )

    for e in range(GROUP - 1):
        pat_copy(e).start()
    for n in range(heads):
        for i in range(2):
            for e in range(GROUP - 1):
                kv_copy(i, n, e).start()
            if n < 2:
                z_start(i, n, role, True)
        for e in range(GROUP - 1):
            q_copy(n, e).start()
    for n in range(heads):
        for c in range(GROUP):
            w_copy(n, c).start()
    h_load.start()

    @pl.when(jnp.logical_not(has_prev))
    def _():
        for n in range(heads):
            kv[:, n, 0 : GROUP * rows, :] = jnp.zeros((2, GROUP * rows, HEAD_DIM), kv.dtype)

    pat_load.wait()
    for e in range(GROUP - 1):
        pat_arrive(peers[e])

    query_place = lax.broadcasted_iota(jnp.int32, (BLOCK, BLOCK), 0)
    key_place = lax.broadcasted_iota(jnp.int32, (BLOCK, BLOCK), 1)
    span_blocks = span // BLOCK
    for c in range(GROUP):
        for i in range(blocks):
            for g in range(span_blocks):
                j = i + WINDOW_BLOCKS - 1 - g
                if j < 0 or j >= WINDOW_BLOCKS:
                    value = jnp.full((BLOCK, BLOCK), HIDE, jnp.float32)
                else:
                    valid = (first_shard + c) * blocks + i - j >= 0
                    floor = jnp.where(valid, 0.0, HIDE).astype(jnp.float32)
                    level = jnp.where(patterns[c, i : i + 1, j : j + 1] == 1, floor, HIDE)
                    value = jnp.broadcast_to(level, (BLOCK, BLOCK))
                    if j == 0:
                        value = jnp.where(key_place <= query_place, value, HIDE)
                bias[c, i * BLOCK : (i + 1) * BLOCK, g * BLOCK : (g + 1) * BLOCK] = value

    factor = math.log2(math.e) / math.sqrt(HEAD_DIM)
    tile = math.gcd(model, 1024)

    def forward(n):
        for i in range(2):
            kv_local(i, n).wait()
        for e in (1, 2, 0):
            for i in range(2):
                kv_arrive(i, n, GROUP + peers[e])
                z_start(i, n, peers[e], False)

        @pl.when(n + 2 < heads)
        def _():
            for i in range(2):
                z_start(i, jnp.minimum(n + 2, heads - 1), role, True)

    def unit(n, c):
        @pl.when(c == role)
        def _():
            q_local(n).wait()

        @pl.when(c != role)
        def _():
            q_arrive(n, c)

        z_arrive(n, c)
        keys_at = pl.ds(c * rows + skip, span)
        query = qbuf[n, c * rows : (c + 1) * rows, :]
        scores = lax.dot_general(
            query, kv[0, n, keys_at, :], (((1,), (1,)), ((), ())),
            preferred_element_type=jnp.float32,
        )
        scores = scores + bias[c]
        largest = jnp.max(scores, axis=1, keepdims=True)
        exponent = jnp.exp2((scores - largest) * factor)
        total = jnp.sum(exponent, axis=1, keepdims=True)
        mixture = jnp.dot(
            exponent.astype(jnp.bfloat16), kv[1, n, keys_at, :],
            preferred_element_type=jnp.float32,
        )
        result = (mixture / total).astype(jnp.bfloat16)

        @pl.when(c == role)
        def _():
            amix[n, :, mix_cols(c)] = result

        @pl.when(c != role)
        def _():
            obuf[n, c * rows : (c + 1) * rows, :] = result
            o_copy(n, c).start()

    def mixed_ready(n):
        for e in range(GROUP - 1):
            o_arrive(n, peers[e])

    def depth(n):
        return pl.ds(pl.multiple_of(n * GROUP * HEAD_DIM, GROUP * HEAD_DIM), GROUP * HEAD_DIM)

    def project(n, first):
        for c in range(GROUP):
            w_copy(n, c).wait()
        mixed_ready(n)
        for t in range(0, model, tile):
            value = jnp.dot(
                amix[n], wbuf[depth(n), t : t + tile], preferred_element_type=jnp.float32
            )
            if first:
                acc[:, t : t + tile] = value
            else:
                acc[:, t : t + tile] += value

    @pl.loop(0, heads)
    def _(t):
        forward(t)

        @pl.when(t >= 1)
        def _():
            for c in reversed(range(GROUP)):
                unit(t - 1, c)

    last_head = heads - 1
    for c in reversed(range(GROUP)):
        unit(last_head, c)
    for n in range(last_head):
        project(n, n == 0)
    h_load.wait()
    for c in range(GROUP):
        w_copy(last_head, c).wait()
    mixed_ready(last_head)

    pieces = part_send.shape[0]
    part_cols = width // pieces

    def part_copy(c):
        cols = pl.ds(c * part_cols, part_cols)
        return pltpu.make_async_remote_copy(
            src_ref=outgoing.at[:, cols],
            dst_ref=incoming.at[:, cols],
            send_sem=part_send.at[c],
            recv_sem=part_recv.at[c],
            device_id={"section": partner},
            device_id_type=MESH,
        )

    def last_sum(start):
        cols = pl.ds(pl.multiple_of(start, part_cols), part_cols)
        return acc[:, cols] + jnp.dot(
            amix[last_head], wbuf[depth(last_head), cols], preferred_element_type=jnp.float32
        )

    for c in range(pieces):
        outgoing[:, c * part_cols : (c + 1) * part_cols] = last_sum(
            partner * width + c * part_cols
        ).astype(outgoing.dtype)
        if c >= 1:
            part_copy(c - 1).start()
    for c in range(pieces):
        cols = slice(c * part_cols, (c + 1) * part_cols)
        mine[:, cols] = last_sum(section * width + c * part_cols).astype(mine.dtype)
        if c == 0:
            part_copy(pieces - 1).start()
    for c in range(pieces):
        part_copy(c).wait_recv()

    strip = 16

    @pl.loop(0, rows // strip)
    def _(i):
        at = pl.ds(pl.multiple_of(i * strip, strip), strip)
        here = mine[at, :].astype(jnp.float32)
        there = incoming[at, :].astype(jnp.float32)
        stream = hbuf[at, :].astype(jnp.float32) + (here + there)
        stream_ref[at, :] = stream
        squares = stream * stream
        lanes = squares[:, 0:128]
        for c in range(128, width, 128):
            lanes = lanes + squares[:, c : c + 128]
        square_out[at, :] = lanes

    square_copy = pltpu.make_async_remote_copy(
        src_ref=square_out,
        dst_ref=square_in,
        send_sem=sq_sem.at[0],
        recv_sem=sq_sem.at[1],
        device_id={"section": partner},
        device_id_type=MESH,
    )
    square_copy.start()

    for e in range(GROUP - 1):
        pat_copy(e).wait_send()

    @pl.loop(0, heads)
    def _(n):
        for e in range(GROUP - 1):
            for i in range(2):
                kv_copy(i, n, e).wait_send()
            q_copy(n, e).wait_send()
            o_copy(n, peers[e]).wait_send()
        for i in range(2):
            for c in range(GROUP):
                z_end(i, n, c)

    for c in range(pieces):
        part_copy(c).wait_send()
    square_copy.wait()
    square_ref[...] = square_out[...] + square_in[...]


def shards(queries, key_rows, value_rows, block_pattern, out_weight, hidden, norm_gain):
    rows, width = queries.shape
    model = out_weight.shape[1]
    heads = width // (GROUP * HEAD_DIM)
    pieces = 4
    span = (WINDOW_BLOCKS - 1) * BLOCK + rows
    anywhere = pl.BlockSpec(memory_space=pl.ANY)
    vmem = pl.BlockSpec(memory_space=pltpu.VMEM)
    bf16 = jnp.bfloat16
    stream, squares = pl.pallas_call(
        kernel,
        out_shape=(
            jax.ShapeDtypeStruct((rows, width), jnp.float32),
            jax.ShapeDtypeStruct((rows, 128), jnp.float32),
        ),
        in_specs=[anywhere] * 6,
        out_specs=(vmem, vmem),
        scratch_shapes=[
            pltpu.VMEM((2, heads, 2 * GROUP * rows, HEAD_DIM), bf16),
            pltpu.VMEM((heads, GROUP * rows, HEAD_DIM), bf16),
            pltpu.VMEM((heads, GROUP * rows, HEAD_DIM), bf16),
            pltpu.VMEM((heads, rows, GROUP * HEAD_DIM), bf16),
            pltpu.VMEM((width, model), bf16),
            pltpu.VMEM((rows, width), bf16),
            pltpu.VMEM((GROUP,) + block_pattern.shape, jnp.int32),
            pltpu.VMEM((GROUP, rows, span), jnp.float32),
            pltpu.VMEM((rows, model), jnp.float32),
            pltpu.VMEM((rows, width), bf16),
            pltpu.VMEM((rows, width), bf16),
            pltpu.VMEM((rows, width), bf16),
            pltpu.VMEM((rows, 128), jnp.float32),
            pltpu.VMEM((rows, 128), jnp.float32),
            pltpu.SemaphoreType.DMA((2, heads)),
            pltpu.SemaphoreType.DMA((heads,)),
            pltpu.SemaphoreType.DMA((1,)),
            pltpu.SemaphoreType.DMA((heads, GROUP)),
            pltpu.SemaphoreType.DMA((1,)),
            pltpu.SemaphoreType.DMA((2, heads, GROUP - 1)),
            pltpu.SemaphoreType.DMA((2, heads, 2 * GROUP)),
            pltpu.SemaphoreType.DMA((2, heads, GROUP)),
            pltpu.SemaphoreType.DMA((heads, GROUP - 1)),
            pltpu.SemaphoreType.DMA((heads, GROUP)),
            pltpu.SemaphoreType.DMA((heads, GROUP)),
            pltpu.SemaphoreType.DMA((heads, GROUP)),
            pltpu.SemaphoreType.DMA((GROUP - 1,)),
            pltpu.SemaphoreType.DMA((GROUP,)),
            pltpu.SemaphoreType.DMA((pieces,)),
            pltpu.SemaphoreType.DMA((pieces,)),
            pltpu.SemaphoreType.DMA((2,)),
        ],
        compiler_params=pltpu.CompilerParams(
            collective_id=0, has_side_effects=True, vmem_limit_bytes=62 * 1024 * 1024
        ),
    )(queries, key_rows, value_rows, block_pattern, out_weight, hidden)
    mean_square = jnp.sum(squares, axis=1, keepdims=True) / model
    normed = stream * lax.rsqrt(mean_square + 1e-06) * norm_gain[None, :]
    return (stream.astype(jnp.bfloat16), normed.astype(jnp.bfloat16))


def solution(mesh):
    placed = (
        P("seq", "section"),
        P("seq", "section"),
        P("seq", "section"),
        P("seq", None),
        P("section", None),
        P("seq", "section"),
        P("section"),
    )
    return jax.shard_map(
        shards,
        mesh=mesh,
        in_specs=placed,
        out_specs=(P("seq", "section"), P("seq", "section")),
        check_vma=False,
    )
```

```python
import math

import jax
import jax.numpy as jnp
from jax import lax
from jax.experimental import pallas as pl
from jax.experimental.pallas import tpu as pltpu
from jax.sharding import PartitionSpec as P

HEAD_DIM = 128
BLOCK = 128
WINDOW_BLOCKS = 8
GROUP = 4
MESH = pl.DeviceIdType.MESH
HIDE = -1e30


def kernel(
    q_hbm, k_hbm, v_hbm, pattern_hbm, w_hbm, h_hbm,
    stream_ref, square_ref,
    kv, qbuf, obuf, amix, wbuf, hbuf, patterns, bias, acc, square_out, square_in,
    kv_own, q_own, pat_own, w_own, w_send, w_recv, h_sem,
    kv_send, kv_recv, z_send, q_send, q_recv, o_send, o_recv, pat_send, pat_recv,
    mix_send, mix_recv, sq_sem, entered,
):
    rows, width = q_hbm.shape
    features = h_hbm.shape[1]
    heads = kv.shape[1]
    blocks = rows // BLOCK
    front = (WINDOW_BLOCKS - 1) * BLOCK
    span = front + rows
    skip = GROUP * rows - front
    shard = lax.axis_index("seq")
    section = lax.axis_index("section")
    count = lax.axis_size("seq")
    role = lax.rem(shard, GROUP)
    first_shard = shard - role
    has_prev = shard >= GROUP
    has_next = shard + GROUP < count
    partner = 1 - section
    low = lax.rem(role, 2)
    high = role // 2
    peers = (3 - role, 2 * high + 1 - low, 2 * (1 - high) + low)
    sources = (k_hbm, v_hbm)

    def head_cols(home, n):
        return pl.ds(pl.multiple_of((home * heads + n) * HEAD_DIM, HEAD_DIM), HEAD_DIM)

    def place(slot):
        return pl.ds(pl.multiple_of(slot * rows, rows), rows)

    def to_peer(peer):
        return {"seq": first_shard + peer}

    def kv_local(i, n):
        return pltpu.make_async_copy(
            sources[i].at[:, head_cols(role, n)],
            kv.at[i, n, place(GROUP + role), :],
            kv_own.at[i, n],
        )

    def q_local(n):
        return pltpu.make_async_copy(
            q_hbm.at[:, head_cols(role, n)], qbuf.at[n, place(role), :], q_own.at[n]
        )

    def kv_copy(i, n, e):
        return pltpu.make_async_remote_copy(
            src_ref=sources[i].at[:, head_cols(peers[e], n)],
            dst_ref=kv.at[i, n, place(GROUP + role), :],
            send_sem=kv_send.at[i, n, e],
            recv_sem=kv_recv.at[i, n, GROUP + role],
            device_id=to_peer(peers[e]),
            device_id_type=MESH,
        )

    def kv_arrive(i, n, slot):
        pltpu.make_async_remote_copy(
            src_ref=kv.at[i, n, place(slot), :],
            dst_ref=kv.at[i, n, place(slot), :],
            send_sem=kv_send.at[i, n, 0],
            recv_sem=kv_recv.at[i, n, slot],
            device_id={"section": partner},
            device_id_type=MESH,
        ).wait_recv()

    def q_copy(n, e):
        return pltpu.make_async_remote_copy(
            src_ref=q_hbm.at[:, head_cols(peers[e], n)],
            dst_ref=qbuf.at[n, place(role), :],
            send_sem=q_send.at[n, e],
            recv_sem=q_recv.at[n, role],
            device_id=to_peer(peers[e]),
            device_id_type=MESH,
        )

    def q_arrive(n, c):
        pltpu.make_async_remote_copy(
            src_ref=qbuf.at[n, place(c), :],
            dst_ref=qbuf.at[n, place(c), :],
            send_sem=q_send.at[n, 0],
            recv_sem=q_recv.at[n, c],
            device_id={"section": partner},
            device_id_type=MESH,
        ).wait_recv()

    def mix_cols(c):
        return pl.ds(pl.multiple_of(c * HEAD_DIM, HEAD_DIM), HEAD_DIM)

    def o_copy(n, c):
        return pltpu.make_async_remote_copy(
            src_ref=obuf.at[n, place(c), :],
            dst_ref=amix.at[0, n, :, mix_cols(role)],
            send_sem=o_send.at[n, c],
            recv_sem=o_recv.at[n, role],
            device_id=to_peer(c),
            device_id_type=MESH,
        )

    def o_arrive(n, c):
        pltpu.make_async_remote_copy(
            src_ref=amix.at[0, n, :, mix_cols(c)],
            dst_ref=amix.at[0, n, :, mix_cols(c)],
            send_sem=o_send.at[n, 0],
            recv_sem=o_recv.at[n, c],
            device_id={"section": partner},
            device_id_type=MESH,
        ).wait_recv()

    def pat_copy(e):
        return pltpu.make_async_remote_copy(
            src_ref=pattern_hbm,
            dst_ref=patterns.at[role],
            send_sem=pat_send.at[e],
            recv_sem=pat_recv.at[role],
            device_id=to_peer(peers[e]),
            device_id_type=MESH,
        )

    def pat_arrive(c):
        pltpu.make_async_remote_copy(
            src_ref=patterns.at[c],
            dst_ref=patterns.at[c],
            send_sem=pat_send.at[0],
            recv_sem=pat_recv.at[c],
            device_id={"section": partner},
            device_id_type=MESH,
        ).wait_recv()

    def z_copies(i, n, c, own):
        def one(first, extent):
            if own:
                source = sources[i].at[pl.ds(first, extent), head_cols(role, n)]
            else:
                source = kv.at[
                    i, n, pl.ds(pl.multiple_of((GROUP + c) * rows + first, BLOCK), extent), :
                ]
            return pltpu.make_async_remote_copy(
                src_ref=source,
                dst_ref=kv.at[i, n, pl.ds(pl.multiple_of(c * rows + first, BLOCK), extent), :],
                send_sem=z_send.at[i, n, c],
                recv_sem=kv_recv.at[i, n, c],
                device_id={"seq": shard + GROUP},
                device_id_type=MESH,
            )

        return one(skip, rows - skip), one(0, rows)

    def z_act(i, n, c, own, act):
        tail, full = z_copies(i, n, c, own)

        @pl.when(has_next & (c == 0))
        def _():
            act(tail)

        @pl.when(has_next & (c > 0))
        def _():
            act(full)

    def z_start(i, n, c, own):
        z_act(i, n, c, own, lambda copy: copy.start())

    def z_end(i, n, c):
        z_act(i, n, c, False, lambda copy: copy.wait_send())

    def z_arrive(n, c):
        @pl.when(has_prev)
        def _():
            for i in range(2):
                tail = pl.ds(c * rows + (skip if c == 0 else 0), rows - (skip if c == 0 else 0))
                pltpu.make_async_remote_copy(
                    src_ref=kv.at[i, n, tail, :],
                    dst_ref=kv.at[i, n, tail, :],
                    send_sem=z_send.at[i, n, 0],
                    recv_sem=kv_recv.at[i, n, c],
                    device_id={"section": partner},
                    device_id_type=MESH,
                ).wait_recv()

    def w_part(n, c, owner):
        return w_hbm.at[
            pl.ds((c * heads + n) * HEAD_DIM, HEAD_DIM),
            pl.ds(pl.multiple_of(owner * features, features), features),
        ]

    def w_local(n, c):
        return pltpu.make_async_copy(
            w_part(n, c, section),
            wbuf.at[0, n, c * HEAD_DIM : (c + 1) * HEAD_DIM, :],
            w_own.at[n, c],
        )

    def w_copy(n, c):
        return pltpu.make_async_remote_copy(
            src_ref=w_part(n, c, partner),
            dst_ref=wbuf.at[1, n, c * HEAD_DIM : (c + 1) * HEAD_DIM, :],
            send_sem=w_send.at[n, c],
            recv_sem=w_recv.at[n, c],
            device_id={"section": partner},
            device_id_type=MESH,
        )

    def mix_copy(n, first, extent):
        cols = pl.ds(first * HEAD_DIM, extent * HEAD_DIM)
        return pltpu.make_async_remote_copy(
            src_ref=amix.at[0, n, :, cols],
            dst_ref=amix.at[1, n, :, cols],
            send_sem=mix_send.at[n, first],
            recv_sem=mix_recv.at[n, first],
            device_id={"section": partner},
            device_id_type=MESH,
        )

    h_load = pltpu.make_async_copy(h_hbm, hbuf, h_sem.at[0])
    pat_load = pltpu.make_async_copy(pattern_hbm, patterns.at[role], pat_own.at[0])

    barrier = pltpu.get_barrier_semaphore()
    for e in range(1, GROUP - 1):
        pl.semaphore_signal(barrier, inc=1, device_id=to_peer(peers[e]), device_id_type=MESH)
    pl.semaphore_signal(barrier, inc=1, device_id={"section": partner}, device_id_type=MESH)

    @pl.when(has_prev)
    def _():
        pl.semaphore_signal(
            barrier, inc=1, device_id={"seq": shard - GROUP}, device_id_type=MESH
        )

    @pl.when(has_next)
    def _():
        pl.semaphore_signal(
            barrier, inc=1, device_id={"seq": shard + GROUP}, device_id_type=MESH
        )

    pat_load.start()
    for n in range(heads):
        for i in range(2):
            kv_local(i, n).start()
        q_local(n).start()

    pl.semaphore_wait(
        barrier, GROUP - 1 + has_prev.astype(jnp.int32) + has_next.astype(jnp.int32)
    )

    pl.semaphore_signal(entered, inc=1, device_id=to_peer(peers[1]), device_id_type=MESH)

    def send(kind, n, e):
        if kind == 2:
            q_copy(n, e).start()
        else:
            kv_copy(kind, n, e).start()

    for e in (1, 2):
        pat_copy(e).start()
        send(0, 0, e)
    z_start(0, 0, role, True)
    z_start(1, 0, role, True)
    pl.semaphore_wait(entered, 1)
    pat_copy(0).start()
    send(0, 0, 0)
    for n in range(heads):
        for kind in range(3):
            if n + kind > 0:
                for e in range(GROUP - 1):
                    send(kind, n, e)
                if n == 1 and kind < 2:
                    z_start(kind, n, role, True)
    for n in range(heads):
        for c in range(GROUP):
            w_copy(n, c).start()
            w_local(n, c).start()
    h_load.start()

    @pl.when(jnp.logical_not(has_prev))
    def _():
        for n in range(heads):
            kv[:, n, 0 : GROUP * rows, :] = jnp.zeros((2, GROUP * rows, HEAD_DIM), kv.dtype)

    pat_load.wait()
    for e in range(GROUP - 1):
        pat_arrive(peers[e])

    query_place = lax.broadcasted_iota(jnp.int32, (BLOCK, BLOCK), 0)
    key_place = lax.broadcasted_iota(jnp.int32, (BLOCK, BLOCK), 1)
    span_blocks = span // BLOCK
    for c in range(GROUP):
        for i in range(blocks):
            for g in range(span_blocks):
                j = i + WINDOW_BLOCKS - 1 - g
                if j < 0 or j >= WINDOW_BLOCKS:
                    value = jnp.full((BLOCK, BLOCK), HIDE, jnp.float32)
                else:
                    valid = (first_shard + c) * blocks + i - j >= 0
                    floor = jnp.where(valid, 0.0, HIDE).astype(jnp.float32)
                    level = jnp.where(patterns[c, i : i + 1, j : j + 1] == 1, floor, HIDE)
                    value = jnp.broadcast_to(level, (BLOCK, BLOCK))
                    if j == 0:
                        value = jnp.where(key_place <= query_place, value, HIDE)
                bias[c, i * BLOCK : (i + 1) * BLOCK, g * BLOCK : (g + 1) * BLOCK] = value

    factor = math.log2(math.e) / math.sqrt(HEAD_DIM)
    tile = math.gcd(features, 512)

    def forward(n):
        for i in range(2):
            for e in (1, 2, 0):
                kv_arrive(i, n, GROUP + peers[e])
                z_start(i, n, peers[e], False)
        for i in range(2):
            kv_local(i, n).wait()

        @pl.when(n + 2 < heads)
        def _():
            for i in range(2):
                z_start(i, jnp.minimum(n + 2, heads - 1), role, True)

    def unit(n, e):
        c = role if e is None else peers[e]
        if e is None:
            q_local(n).wait()
        else:
            q_arrive(n, c)
        keys_at = pl.ds(pl.multiple_of(c * rows + skip, BLOCK), span)
        query = qbuf[n, place(c), :]
        scores = lax.dot_general(
            query, kv[0, n, keys_at, :], (((1,), (1,)), ((), ())),
            preferred_element_type=jnp.float32,
        )
        scores = scores + bias[c]
        largest = jnp.max(scores, axis=1, keepdims=True)
        exponent = jnp.exp2((scores - largest) * factor)
        total = jnp.sum(exponent, axis=1, keepdims=True)
        mixture = jnp.dot(
            exponent.astype(jnp.bfloat16), kv[1, n, keys_at, :],
            preferred_element_type=jnp.float32,
        )
        result = (mixture / total).astype(jnp.bfloat16)

        if e is None:
            amix[0, n, :, mix_cols(c)] = result
        else:
            obuf[n, place(c), :] = result
            o_copy(n, c).start()

    def project_own(n, first):
        for e in range(GROUP - 1):
            o_arrive(n, peers[e])
        mix_copy(n, 0, GROUP).start()
        for c in range(GROUP):
            w_local(n, c).wait()
        for t in range(0, features, tile):
            value = jnp.dot(
                amix[0, n], wbuf[0, n, :, t : t + tile], preferred_element_type=jnp.float32
            )
            if first:
                acc[:, t : t + tile] = value
            else:
                acc[:, t : t + tile] += value

    def project_other(n):
        for c in range(GROUP):
            w_copy(n, c).wait_recv()
        mix_copy(n, 0, GROUP).wait_recv()
        for t in range(0, features, tile):
            acc[:, t : t + tile] += jnp.dot(
                amix[1, n], wbuf[1, n, :, t : t + tile], preferred_element_type=jnp.float32
            )

    last = heads - 1

    def chunk(n):
        for c in reversed(range(GROUP)):
            z_arrive(n, c)
        for e in range(GROUP - 1):
            unit(n, e)

    @pl.loop(0, heads)
    def _(n):
        forward(n)

        @pl.when(n >= 1)
        def _():
            chunk(n - 1)
            unit(n - 1, None)

    project_own(0, True)
    chunk(last)
    if last > 1:
        project_own(1, False)
    project_other(0)
    unit(last, None)
    for n in range(1, last):
        if n > 1:
            project_own(n, False)
        project_other(n)
    h_load.wait()

    for c in range(GROUP):
        w_local(last, c).wait()
        w_copy(last, c).wait_recv()

        @pl.when(c != role)
        def _():
            o_arrive(last, c)

        mix_copy(last, c, 1).start()
    for t in range(0, features, tile):
        acc[:, t : t + tile] += jnp.dot(
            amix[0, last], wbuf[0, last, :, t : t + tile], preferred_element_type=jnp.float32
        )
    for c in range(GROUP):
        mix_copy(last, c, 1).wait_recv()
    lanes = jnp.zeros(square_out.shape, jnp.float32)
    for t in range(0, features, tile):
        value = acc[:, t : t + tile] + jnp.dot(
            amix[1, last], wbuf[1, last, :, t : t + tile], preferred_element_type=jnp.float32
        )
        stream = hbuf[:, t : t + tile].astype(jnp.float32) + value
        stream_ref[:, t : t + tile] = stream
        squares = stream * stream
        for p in range(0, tile, 128):
            lanes = lanes + squares[:, p : p + 128]
    square_out[...] = lanes

    square_copy = pltpu.make_async_remote_copy(
        src_ref=square_out,
        dst_ref=square_in,
        send_sem=sq_sem.at[0],
        recv_sem=sq_sem.at[1],
        device_id={"section": partner},
        device_id_type=MESH,
    )
    square_copy.start()

    for e in range(GROUP - 1):
        pat_copy(e).wait_send()

    @pl.loop(0, heads)
    def _(n):
        for e in range(GROUP - 1):
            for i in range(2):
                kv_copy(i, n, e).wait_send()
            q_copy(n, e).wait_send()
            o_copy(n, peers[e]).wait_send()
        for i in range(2):
            for c in range(GROUP):
                z_end(i, n, c)

    for n in range(heads):
        for c in range(GROUP):
            w_copy(n, c).wait_send()
            if n == last:
                mix_copy(n, c, 1).wait_send()
        if n < last:
            mix_copy(n, 0, GROUP).wait_send()
    square_copy.wait()
    square_ref[...] = square_out[...] + square_in[...]


def shards(queries, key_rows, value_rows, block_pattern, out_weight, hidden, norm_gain):
    rows, width = queries.shape
    model = out_weight.shape[1]
    heads = width // (GROUP * HEAD_DIM)
    features = hidden.shape[1]
    span = (WINDOW_BLOCKS - 1) * BLOCK + rows
    anywhere = pl.BlockSpec(memory_space=pl.ANY)
    vmem = pl.BlockSpec(memory_space=pltpu.VMEM)
    bf16 = jnp.bfloat16
    stream, squares = pl.pallas_call(
        kernel,
        out_shape=(
            jax.ShapeDtypeStruct((rows, features), jnp.float32),
            jax.ShapeDtypeStruct((rows, 128), jnp.float32),
        ),
        in_specs=[anywhere] * 6,
        out_specs=(vmem, vmem),
        scratch_shapes=[
            pltpu.VMEM((2, heads, 2 * GROUP * rows, HEAD_DIM), bf16),
            pltpu.VMEM((heads, GROUP * rows, HEAD_DIM), bf16),
            pltpu.VMEM((heads, GROUP * rows, HEAD_DIM), bf16),
            pltpu.VMEM((2, heads, rows, GROUP * HEAD_DIM), bf16),
            pltpu.VMEM((2, heads, GROUP * HEAD_DIM, features), bf16),
            pltpu.VMEM((rows, features), bf16),
            pltpu.VMEM((GROUP,) + block_pattern.shape, jnp.int32),
            pltpu.VMEM((GROUP, rows, span), jnp.float32),
            pltpu.VMEM((rows, features), jnp.float32),
            pltpu.VMEM((rows, 128), jnp.float32),
            pltpu.VMEM((rows, 128), jnp.float32),
            pltpu.SemaphoreType.DMA((2, heads)),
            pltpu.SemaphoreType.DMA((heads,)),
            pltpu.SemaphoreType.DMA((1,)),
            pltpu.SemaphoreType.DMA((heads, GROUP)),
            pltpu.SemaphoreType.DMA((heads, GROUP)),
            pltpu.SemaphoreType.DMA((heads, GROUP)),
            pltpu.SemaphoreType.DMA((1,)),
            pltpu.SemaphoreType.DMA((2, heads, GROUP - 1)),
            pltpu.SemaphoreType.DMA((2, heads, 2 * GROUP)),
            pltpu.SemaphoreType.DMA((2, heads, GROUP)),
            pltpu.SemaphoreType.DMA((heads, GROUP - 1)),
            pltpu.SemaphoreType.DMA((heads, GROUP)),
            pltpu.SemaphoreType.DMA((heads, GROUP)),
            pltpu.SemaphoreType.DMA((heads, GROUP)),
            pltpu.SemaphoreType.DMA((GROUP - 1,)),
            pltpu.SemaphoreType.DMA((GROUP,)),
            pltpu.SemaphoreType.DMA((heads, GROUP)),
            pltpu.SemaphoreType.DMA((heads, GROUP)),
            pltpu.SemaphoreType.DMA((2,)),
            pltpu.SemaphoreType.REGULAR,
        ],
        compiler_params=pltpu.CompilerParams(
            collective_id=0, has_side_effects=True, vmem_limit_bytes=40 * 1024 * 1024
        ),
    )(
        *[
            pltpu.with_memory_space_constraint(value, pltpu.HBM)
            for value in (
                queries, key_rows, value_rows, block_pattern, out_weight, hidden
            )
        ]
    )
    mean_square = jnp.sum(squares, axis=1, keepdims=True) / model
    normed = stream * lax.rsqrt(mean_square + 1e-06) * norm_gain[None, :]
    return (stream.astype(jnp.bfloat16), normed.astype(jnp.bfloat16))


def solution(mesh):
    placed = (
        P("seq", "section"),
        P("seq", "section"),
        P("seq", "section"),
        P("seq", None),
        P("section", None),
        P("seq", "section"),
        P("section"),
    )
    return jax.shard_map(
        shards,
        mesh=mesh,
        in_specs=placed,
        out_specs=(P("seq", "section"), P("seq", "section")),
        check_vma=False,
    )
```

```python
import math

import jax
import jax.numpy as jnp
from jax import lax
from jax.experimental import pallas as pl
from jax.experimental.pallas import tpu as pltpu
from jax.sharding import PartitionSpec as P

HEAD_DIM = 128
BLOCK = 128
WINDOW_BLOCKS = 8
GROUP = 4
MESH = pl.DeviceIdType.MESH
HIDE = -1e30


def kernel(
    q_hbm, k_hbm, v_hbm, pattern_hbm, w_hbm, h_hbm,
    stream_ref, square_ref,
    kv, qbuf, obuf, amix, wbuf, hbuf, patterns, bias, acc, square_out, square_in,
    kv_own, q_own, pat_own, w_own, w_send, w_recv, h_sem,
    kv_send, kv_recv, z_send, q_send, q_recv, o_send, o_recv, pat_send, pat_recv,
    mix_send, mix_recv, sq_sem, entered,
):
    rows, width = q_hbm.shape
    features = h_hbm.shape[1]
    heads = kv.shape[1]
    blocks = rows // BLOCK
    front = (WINDOW_BLOCKS - 1) * BLOCK
    span = front + rows
    skip = GROUP * rows - front
    shard = lax.axis_index("seq")
    section = lax.axis_index("section")
    count = lax.axis_size("seq")
    role = lax.rem(shard, GROUP)
    first_shard = shard - role
    has_prev = shard >= GROUP
    has_next = shard + GROUP < count
    partner = 1 - section
    low = lax.rem(role, 2)
    high = role // 2
    peers = (3 - role, 2 * high + 1 - low, 2 * (1 - high) + low)
    sources = (k_hbm, v_hbm)

    def head_cols(home, n):
        return pl.ds(pl.multiple_of((home * heads + n) * HEAD_DIM, HEAD_DIM), HEAD_DIM)

    def place(slot):
        return pl.ds(pl.multiple_of(slot * rows, rows), rows)

    def to_peer(peer):
        return {"seq": first_shard + peer}

    def kv_local(i, n):
        return pltpu.make_async_copy(
            sources[i].at[:, head_cols(role, n)],
            kv.at[i, n, place(GROUP + role), :],
            kv_own.at[i, n],
        )

    def q_local(n):
        return pltpu.make_async_copy(
            q_hbm.at[:, head_cols(role, n)], qbuf.at[n, place(role), :], q_own.at[n]
        )

    def kv_copy(i, n, e):
        return pltpu.make_async_remote_copy(
            src_ref=sources[i].at[:, head_cols(peers[e], n)],
            dst_ref=kv.at[i, n, place(GROUP + role), :],
            send_sem=kv_send.at[i, n, e],
            recv_sem=kv_recv.at[i, n, GROUP + role],
            device_id=to_peer(peers[e]),
            device_id_type=MESH,
        )

    def kv_arrive(i, n, slot):
        pltpu.make_async_remote_copy(
            src_ref=kv.at[i, n, place(slot), :],
            dst_ref=kv.at[i, n, place(slot), :],
            send_sem=kv_send.at[i, n, 0],
            recv_sem=kv_recv.at[i, n, slot],
            device_id={"section": partner},
            device_id_type=MESH,
        ).wait_recv()

    def q_copy(n, e):
        return pltpu.make_async_remote_copy(
            src_ref=q_hbm.at[:, head_cols(peers[e], n)],
            dst_ref=qbuf.at[n, place(role), :],
            send_sem=q_send.at[n, e],
            recv_sem=q_recv.at[n, role],
            device_id=to_peer(peers[e]),
            device_id_type=MESH,
        )

    def q_arrive(n, c):
        pltpu.make_async_remote_copy(
            src_ref=qbuf.at[n, place(c), :],
            dst_ref=qbuf.at[n, place(c), :],
            send_sem=q_send.at[n, 0],
            recv_sem=q_recv.at[n, c],
            device_id={"section": partner},
            device_id_type=MESH,
        ).wait_recv()

    def mix_cols(c):
        return pl.ds(pl.multiple_of(c * HEAD_DIM, HEAD_DIM), HEAD_DIM)

    def o_copy(n, c):
        return pltpu.make_async_remote_copy(
            src_ref=obuf.at[n, place(c), :],
            dst_ref=amix.at[0, n, :, mix_cols(role)],
            send_sem=o_send.at[n, c],
            recv_sem=o_recv.at[n, role],
            device_id=to_peer(c),
            device_id_type=MESH,
        )

    def o_arrive(n, c):
        pltpu.make_async_remote_copy(
            src_ref=amix.at[0, n, :, mix_cols(c)],
            dst_ref=amix.at[0, n, :, mix_cols(c)],
            send_sem=o_send.at[n, 0],
            recv_sem=o_recv.at[n, c],
            device_id={"section": partner},
            device_id_type=MESH,
        ).wait_recv()

    def pat_copy(e):
        return pltpu.make_async_remote_copy(
            src_ref=pattern_hbm,
            dst_ref=patterns.at[role],
            send_sem=pat_send.at[e],
            recv_sem=pat_recv.at[role],
            device_id=to_peer(peers[e]),
            device_id_type=MESH,
        )

    def pat_arrive(c):
        pltpu.make_async_remote_copy(
            src_ref=patterns.at[c],
            dst_ref=patterns.at[c],
            send_sem=pat_send.at[0],
            recv_sem=pat_recv.at[c],
            device_id={"section": partner},
            device_id_type=MESH,
        ).wait_recv()

    def z_copies(i, n, c, own):
        def one(first, extent):
            if own:
                source = sources[i].at[pl.ds(first, extent), head_cols(role, n)]
            else:
                source = kv.at[
                    i, n, pl.ds(pl.multiple_of((GROUP + c) * rows + first, BLOCK), extent), :
                ]
            return pltpu.make_async_remote_copy(
                src_ref=source,
                dst_ref=kv.at[i, n, pl.ds(pl.multiple_of(c * rows + first, BLOCK), extent), :],
                send_sem=z_send.at[i, n, c],
                recv_sem=kv_recv.at[i, n, c],
                device_id={"seq": shard + GROUP},
                device_id_type=MESH,
            )

        return one(skip, rows - skip), one(0, rows)

    def z_act(i, n, c, own, act):
        tail, full = z_copies(i, n, c, own)

        @pl.when(has_next & (c == 0))
        def _():
            act(tail)

        @pl.when(has_next & (c > 0))
        def _():
            act(full)

    def z_start(i, n, c, own):
        z_act(i, n, c, own, lambda copy: copy.start())

    def z_end(i, n, c):
        z_act(i, n, c, False, lambda copy: copy.wait_send())

    def z_arrive(n, c):
        @pl.when(has_prev)
        def _():
            for i in range(2):
                tail = pl.ds(c * rows + (skip if c == 0 else 0), rows - (skip if c == 0 else 0))
                pltpu.make_async_remote_copy(
                    src_ref=kv.at[i, n, tail, :],
                    dst_ref=kv.at[i, n, tail, :],
                    send_sem=z_send.at[i, n, 0],
                    recv_sem=kv_recv.at[i, n, c],
                    device_id={"section": partner},
                    device_id_type=MESH,
                ).wait_recv()

    def w_part(n, c, owner):
        return w_hbm.at[
            pl.ds((c * heads + n) * HEAD_DIM, HEAD_DIM),
            pl.ds(pl.multiple_of(owner * features, features), features),
        ]

    def w_local(n, c):
        return pltpu.make_async_copy(
            w_part(n, c, section),
            wbuf.at[0, n, c * HEAD_DIM : (c + 1) * HEAD_DIM, :],
            w_own.at[n, c],
        )

    def w_copy(n, c):
        return pltpu.make_async_remote_copy(
            src_ref=w_part(n, c, partner),
            dst_ref=wbuf.at[1, n, c * HEAD_DIM : (c + 1) * HEAD_DIM, :],
            send_sem=w_send.at[n, c],
            recv_sem=w_recv.at[n, c],
            device_id={"section": partner},
            device_id_type=MESH,
        )

    def mix_copy(n, first, extent):
        cols = pl.ds(pl.multiple_of(first * HEAD_DIM, HEAD_DIM), extent * HEAD_DIM)
        return pltpu.make_async_remote_copy(
            src_ref=amix.at[0, n, :, cols],
            dst_ref=amix.at[1, n, :, cols],
            send_sem=mix_send.at[n, first],
            recv_sem=mix_recv.at[n, first],
            device_id={"section": partner},
            device_id_type=MESH,
        )

    h_load = pltpu.make_async_copy(h_hbm, hbuf, h_sem.at[0])
    pat_load = pltpu.make_async_copy(pattern_hbm, patterns.at[role], pat_own.at[0])

    barrier = pltpu.get_barrier_semaphore()
    for e in range(1, GROUP - 1):
        pl.semaphore_signal(barrier, inc=1, device_id=to_peer(peers[e]), device_id_type=MESH)
    pl.semaphore_signal(barrier, inc=1, device_id={"section": partner}, device_id_type=MESH)

    @pl.when(has_prev)
    def _():
        pl.semaphore_signal(
            barrier, inc=1, device_id={"seq": shard - GROUP}, device_id_type=MESH
        )

    @pl.when(has_next)
    def _():
        pl.semaphore_signal(
            barrier, inc=1, device_id={"seq": shard + GROUP}, device_id_type=MESH
        )

    pat_load.start()
    for n in range(heads):
        for i in range(2):
            kv_local(i, n).start()
        q_local(n).start()

    pl.semaphore_wait(
        barrier, GROUP - 1 + has_prev.astype(jnp.int32) + has_next.astype(jnp.int32)
    )

    pl.semaphore_signal(entered, inc=1, device_id=to_peer(peers[1]), device_id_type=MESH)

    def send(kind, n, e):
        if kind == 2:
            q_copy(n, e).start()
        else:
            kv_copy(kind, n, e).start()

    for e in (1, 2):
        pat_copy(e).start()
        send(0, 0, e)
    z_start(0, 0, role, True)
    z_start(1, 0, role, True)
    pl.semaphore_wait(entered, 1)
    pat_copy(0).start()
    send(0, 0, 0)
    for n in range(heads):
        for kind in range(3):
            if n + kind > 0:
                for e in range(GROUP - 1):
                    send(kind, n, e)
                if n == 1 and kind < 2:
                    z_start(kind, n, role, True)
    for n in range(heads):
        for c in range(GROUP):
            w_copy(n, c).start()
            w_local(n, c).start()
    h_load.start()

    @pl.when(jnp.logical_not(has_prev))
    def _():
        for n in range(heads):
            kv[:, n, 0 : GROUP * rows, :] = jnp.zeros((2, GROUP * rows, HEAD_DIM), kv.dtype)

    pat_load.wait()
    for e in range(GROUP - 1):
        pat_arrive(peers[e])

    query_place = lax.broadcasted_iota(jnp.int32, (BLOCK, BLOCK), 0)
    key_place = lax.broadcasted_iota(jnp.int32, (BLOCK, BLOCK), 1)
    span_blocks = span // BLOCK
    for c in range(GROUP):
        for i in range(blocks):
            for g in range(span_blocks):
                j = i + WINDOW_BLOCKS - 1 - g
                if j < 0 or j >= WINDOW_BLOCKS:
                    value = jnp.full((BLOCK, BLOCK), HIDE, jnp.float32)
                else:
                    valid = (first_shard + c) * blocks + i - j >= 0
                    floor = jnp.where(valid, 0.0, HIDE).astype(jnp.float32)
                    level = jnp.where(patterns[c, i : i + 1, j : j + 1] == 1, floor, HIDE)
                    value = jnp.broadcast_to(level, (BLOCK, BLOCK))
                    if j == 0:
                        value = jnp.where(key_place <= query_place, value, HIDE)
                bias[c, i * BLOCK : (i + 1) * BLOCK, g * BLOCK : (g + 1) * BLOCK] = value

    factor = math.log2(math.e) / math.sqrt(HEAD_DIM)
    tile = math.gcd(features, 512)

    def forward(n):
        for i in range(2):
            for e in (1, 2, 0):
                kv_arrive(i, n, GROUP + peers[e])
                z_start(i, n, peers[e], False)
        for i in range(2):
            kv_local(i, n).wait()

        @pl.when(n + 2 < heads)
        def _():
            for i in range(2):
                z_start(i, jnp.minimum(n + 2, heads - 1), role, True)

    def attend(n, c):
        keys_at = pl.ds(pl.multiple_of(c * rows + skip, BLOCK), span)
        scores = lax.dot_general(
            qbuf[n, place(c), :], kv[0, n, keys_at, :], (((1,), (1,)), ((), ())),
            preferred_element_type=jnp.float32,
        )
        scores = scores + bias[c]
        largest = jnp.max(scores, axis=1, keepdims=True)
        exponent = jnp.exp2((scores - largest) * factor)
        total = jnp.sum(exponent, axis=1, keepdims=True)
        mixture = jnp.dot(
            exponent.astype(jnp.bfloat16), kv[1, n, keys_at, :],
            preferred_element_type=jnp.float32,
        )
        return (mixture / total).astype(jnp.bfloat16)

    def units(n, chosen):
        for e in chosen:
            if e is None:
                q_local(n).wait()
            else:
                q_arrive(n, peers[e])
        results = [attend(n, role if e is None else peers[e]) for e in chosen]
        for e, result in zip(chosen, results):
            if e is None:
                amix[0, n, :, mix_cols(role)] = result
            else:
                obuf[n, place(peers[e]), :] = result
        for e in chosen:
            if e is not None:
                o_copy(n, peers[e]).start()

    def project_own(n, first):
        for e in range(GROUP - 1):
            o_arrive(n, peers[e])
        mix_copy(n, 0, GROUP).start()
        for c in range(GROUP):
            w_local(n, c).wait()
        for t in range(0, features, tile):
            value = jnp.dot(
                amix[0, n], wbuf[0, n, :, t : t + tile], preferred_element_type=jnp.float32
            )
            if first:
                acc[:, t : t + tile] = value
            else:
                acc[:, t : t + tile] += value

    def project_other(n):
        for c in range(GROUP):
            w_copy(n, c).wait_recv()
        mix_copy(n, 0, GROUP).wait_recv()
        for t in range(0, features, tile):
            acc[:, t : t + tile] += jnp.dot(
                amix[1, n], wbuf[1, n, :, t : t + tile], preferred_element_type=jnp.float32
            )

    last = heads - 1

    def chunk(n):
        for c in reversed(range(GROUP)):
            z_arrive(n, c)
        for e in (0, 1, 2, None):
            units(n, (e,))

    @pl.loop(0, heads)
    def _(n):
        forward(n)

        @pl.when(n >= 1)
        def _():
            chunk(n - 1)

    project_own(0, True)
    chunk(last)
    mix_copy(last, role, 1).start()
    project_other(0)
    for n in range(1, last):
        project_own(n, False)
        if n > 1:
            project_other(n - 1)
    h_load.wait()
    for c in range(GROUP):
        w_local(last, c).wait()
        w_copy(last, c).wait_recv()
    for e in range(GROUP - 1):
        o_arrive(last, peers[e])
        mix_copy(last, peers[e], 1).start()
    if last > 1:
        project_other(last - 1)
    for t in range(0, features, tile):
        acc[:, t : t + tile] += jnp.dot(
            amix[0, last], wbuf[0, last, :, t : t + tile], preferred_element_type=jnp.float32
        )
    for c in range(GROUP):
        mix_copy(last, c, 1).wait_recv()
    lanes = jnp.zeros(square_out.shape, jnp.float32)
    for t in range(0, features, tile):
        value = acc[:, t : t + tile] + jnp.dot(
            amix[1, last], wbuf[1, last, :, t : t + tile], preferred_element_type=jnp.float32
        )
        stream = hbuf[:, t : t + tile].astype(jnp.float32) + value
        stream_ref[:, t : t + tile] = stream
        squares = stream * stream
        for p in range(0, tile, 128):
            lanes = lanes + squares[:, p : p + 128]
    square_out[...] = lanes

    square_copy = pltpu.make_async_remote_copy(
        src_ref=square_out,
        dst_ref=square_in,
        send_sem=sq_sem.at[0],
        recv_sem=sq_sem.at[1],
        device_id={"section": partner},
        device_id_type=MESH,
    )
    square_copy.start()

    for e in range(GROUP - 1):
        pat_copy(e).wait_send()

    @pl.loop(0, heads)
    def _(n):
        for e in range(GROUP - 1):
            for i in range(2):
                kv_copy(i, n, e).wait_send()
            q_copy(n, e).wait_send()
            o_copy(n, peers[e]).wait_send()
        for i in range(2):
            for c in range(GROUP):
                z_end(i, n, c)

    for n in range(heads):
        for c in range(GROUP):
            w_copy(n, c).wait_send()
            if n == last:
                mix_copy(n, c, 1).wait_send()
        if n < last:
            mix_copy(n, 0, GROUP).wait_send()
    square_copy.wait()
    square_ref[...] = square_out[...] + square_in[...]


def shards(queries, key_rows, value_rows, block_pattern, out_weight, hidden, norm_gain):
    rows, width = queries.shape
    model = out_weight.shape[1]
    heads = width // (GROUP * HEAD_DIM)
    features = hidden.shape[1]
    span = (WINDOW_BLOCKS - 1) * BLOCK + rows
    anywhere = pl.BlockSpec(memory_space=pl.ANY)
    vmem = pl.BlockSpec(memory_space=pltpu.VMEM)
    bf16 = jnp.bfloat16
    stream, squares = pl.pallas_call(
        kernel,
        out_shape=(
            jax.ShapeDtypeStruct((rows, features), jnp.float32),
            jax.ShapeDtypeStruct((rows, 128), jnp.float32),
        ),
        in_specs=[anywhere] * 6,
        out_specs=(vmem, vmem),
        scratch_shapes=[
            pltpu.VMEM((2, heads, 2 * GROUP * rows, HEAD_DIM), bf16),
            pltpu.VMEM((heads, GROUP * rows, HEAD_DIM), bf16),
            pltpu.VMEM((heads, GROUP * rows, HEAD_DIM), bf16),
            pltpu.VMEM((2, heads, rows, GROUP * HEAD_DIM), bf16),
            pltpu.VMEM((2, heads, GROUP * HEAD_DIM, features), bf16),
            pltpu.VMEM((rows, features), bf16),
            pltpu.VMEM((GROUP,) + block_pattern.shape, jnp.int32),
            pltpu.VMEM((GROUP, rows, span), jnp.float32),
            pltpu.VMEM((rows, features), jnp.float32),
            pltpu.VMEM((rows, 128), jnp.float32),
            pltpu.VMEM((rows, 128), jnp.float32),
            pltpu.SemaphoreType.DMA((2, heads)),
            pltpu.SemaphoreType.DMA((heads,)),
            pltpu.SemaphoreType.DMA((1,)),
            pltpu.SemaphoreType.DMA((heads, GROUP)),
            pltpu.SemaphoreType.DMA((heads, GROUP)),
            pltpu.SemaphoreType.DMA((heads, GROUP)),
            pltpu.SemaphoreType.DMA((1,)),
            pltpu.SemaphoreType.DMA((2, heads, GROUP - 1)),
            pltpu.SemaphoreType.DMA((2, heads, 2 * GROUP)),
            pltpu.SemaphoreType.DMA((2, heads, GROUP)),
            pltpu.SemaphoreType.DMA((heads, GROUP - 1)),
            pltpu.SemaphoreType.DMA((heads, GROUP)),
            pltpu.SemaphoreType.DMA((heads, GROUP)),
            pltpu.SemaphoreType.DMA((heads, GROUP)),
            pltpu.SemaphoreType.DMA((GROUP - 1,)),
            pltpu.SemaphoreType.DMA((GROUP,)),
            pltpu.SemaphoreType.DMA((heads, GROUP)),
            pltpu.SemaphoreType.DMA((heads, GROUP)),
            pltpu.SemaphoreType.DMA((2,)),
            pltpu.SemaphoreType.REGULAR,
        ],
        compiler_params=pltpu.CompilerParams(
            collective_id=0, has_side_effects=True, vmem_limit_bytes=40 * 1024 * 1024
        ),
    )(
        *[
            pltpu.with_memory_space_constraint(value, pltpu.HBM)
            for value in (
                queries, key_rows, value_rows, block_pattern, out_weight, hidden
            )
        ]
    )
    mean_square = jnp.sum(squares, axis=1, keepdims=True) / model
    normed = stream * lax.rsqrt(mean_square + 1e-06) * norm_gain[None, :]
    return (stream.astype(jnp.bfloat16), normed.astype(jnp.bfloat16))


def solution(mesh):
    placed = (
        P("seq", "section"),
        P("seq", "section"),
        P("seq", "section"),
        P("seq", None),
        P("section", None),
        P("seq", "section"),
        P("section"),
    )
    return jax.shard_map(
        shards,
        mesh=mesh,
        in_specs=placed,
        out_specs=(P("seq", "section"), P("seq", "section")),
        check_vma=False,
    )
```

```python
import math

import jax
import jax.numpy as jnp
from jax import lax
from jax.experimental import pallas as pl
from jax.experimental.pallas import tpu as pltpu
from jax.sharding import PartitionSpec as P

HEAD_DIM = 128
BLOCK = 128
WINDOW_BLOCKS = 8
GROUP = 4
MESH = pl.DeviceIdType.MESH
HIDE = -1e30


def kernel(
    q_hbm, k_hbm, v_hbm, pattern_hbm, w_hbm, h_hbm,
    stream_ref, square_ref,
    kv, qbuf, obuf, amix, wbuf, hbuf, patterns, bias, acc, square_out, square_in,
    kv_own, q_own, pat_own, w_own, w_send, w_recv, h_sem,
    kv_send, kv_recv, z_send, q_send, q_recv, o_send, o_recv, pat_send, pat_recv,
    mix_send, mix_recv, sq_sem, entered,
):
    rows, width = q_hbm.shape
    features = h_hbm.shape[1]
    heads = kv.shape[1]
    blocks = rows // BLOCK
    front = (WINDOW_BLOCKS - 1) * BLOCK
    span = front + rows
    skip = GROUP * rows - front
    shard = lax.axis_index("seq")
    section = lax.axis_index("section")
    count = lax.axis_size("seq")
    role = lax.rem(shard, GROUP)
    first_shard = shard - role
    has_prev = shard >= GROUP
    has_next = shard + GROUP < count
    partner = 1 - section
    low = lax.rem(role, 2)
    high = role // 2
    peers = (3 - role, 2 * high + 1 - low, 2 * (1 - high) + low)
    sources = (k_hbm, v_hbm)

    def head_cols(home, n):
        return pl.ds(pl.multiple_of((home * heads + n) * HEAD_DIM, HEAD_DIM), HEAD_DIM)

    def place(slot):
        return pl.ds(pl.multiple_of(slot * rows, rows), rows)

    def to_peer(peer):
        return {"seq": first_shard + peer}

    def kv_local(i, n):
        return pltpu.make_async_copy(
            sources[i].at[:, head_cols(role, n)],
            kv.at[i, n, place(GROUP + role), :],
            kv_own.at[i, n],
        )

    def q_local(n):
        return pltpu.make_async_copy(
            q_hbm.at[:, head_cols(role, n)], qbuf.at[n, place(role), :], q_own.at[n]
        )

    def kv_copy(i, n, e):
        return pltpu.make_async_remote_copy(
            src_ref=sources[i].at[:, head_cols(peers[e], n)],
            dst_ref=kv.at[i, n, place(GROUP + role), :],
            send_sem=kv_send.at[i, n, e],
            recv_sem=kv_recv.at[i, n, GROUP + role],
            device_id=to_peer(peers[e]),
            device_id_type=MESH,
        )

    def kv_arrive(i, n, slot):
        pltpu.make_async_remote_copy(
            src_ref=kv.at[i, n, place(slot), :],
            dst_ref=kv.at[i, n, place(slot), :],
            send_sem=kv_send.at[i, n, 0],
            recv_sem=kv_recv.at[i, n, slot],
            device_id={"section": partner},
            device_id_type=MESH,
        ).wait_recv()

    def q_copy(n, e):
        return pltpu.make_async_remote_copy(
            src_ref=q_hbm.at[:, head_cols(peers[e], n)],
            dst_ref=qbuf.at[n, place(role), :],
            send_sem=q_send.at[n, e],
            recv_sem=q_recv.at[n, role],
            device_id=to_peer(peers[e]),
            device_id_type=MESH,
        )

    def q_arrive(n, c):
        pltpu.make_async_remote_copy(
            src_ref=qbuf.at[n, place(c), :],
            dst_ref=qbuf.at[n, place(c), :],
            send_sem=q_send.at[n, 0],
            recv_sem=q_recv.at[n, c],
            device_id={"section": partner},
            device_id_type=MESH,
        ).wait_recv()

    def mixed(k, n, c, extent=1):
        start = ((2 * n + k) * GROUP + c) * HEAD_DIM
        return pl.ds(pl.multiple_of(start, HEAD_DIM), extent * HEAD_DIM)

    def o_copy(n, c):
        return pltpu.make_async_remote_copy(
            src_ref=obuf.at[n, place(c), :],
            dst_ref=amix.at[:, mixed(0, n, role)],
            send_sem=o_send.at[n, c],
            recv_sem=o_recv.at[n, role],
            device_id=to_peer(c),
            device_id_type=MESH,
        )

    def o_arrive(n, c):
        pltpu.make_async_remote_copy(
            src_ref=amix.at[:, mixed(0, n, c)],
            dst_ref=amix.at[:, mixed(0, n, c)],
            send_sem=o_send.at[n, 0],
            recv_sem=o_recv.at[n, c],
            device_id={"section": partner},
            device_id_type=MESH,
        ).wait_recv()

    def pat_copy(e):
        return pltpu.make_async_remote_copy(
            src_ref=pattern_hbm,
            dst_ref=patterns.at[role],
            send_sem=pat_send.at[e],
            recv_sem=pat_recv.at[role],
            device_id=to_peer(peers[e]),
            device_id_type=MESH,
        )

    def pat_arrive(c):
        pltpu.make_async_remote_copy(
            src_ref=patterns.at[c],
            dst_ref=patterns.at[c],
            send_sem=pat_send.at[0],
            recv_sem=pat_recv.at[c],
            device_id={"section": partner},
            device_id_type=MESH,
        ).wait_recv()

    def z_copies(i, n, c, own):
        def one(first, extent):
            if own:
                source = sources[i].at[pl.ds(first, extent), head_cols(role, n)]
            else:
                source = kv.at[
                    i, n, pl.ds(pl.multiple_of((GROUP + c) * rows + first, BLOCK), extent), :
                ]
            return pltpu.make_async_remote_copy(
                src_ref=source,
                dst_ref=kv.at[i, n, pl.ds(pl.multiple_of(c * rows + first, BLOCK), extent), :],
                send_sem=z_send.at[i, n, c],
                recv_sem=kv_recv.at[i, n, c],
                device_id={"seq": shard + GROUP},
                device_id_type=MESH,
            )

        return one(skip, rows - skip), one(0, rows)

    def z_act(i, n, c, own, act):
        tail, full = z_copies(i, n, c, own)

        @pl.when(has_next & (c == 0))
        def _():
            act(tail)

        @pl.when(has_next & (c > 0))
        def _():
            act(full)

    def z_start(i, n, c, own):
        z_act(i, n, c, own, lambda copy: copy.start())

    def z_end(i, n, c):
        z_act(i, n, c, False, lambda copy: copy.wait_send())

    def z_arrive(n, c):
        @pl.when(has_prev)
        def _():
            for i in range(2):
                tail = pl.ds(c * rows + (skip if c == 0 else 0), rows - (skip if c == 0 else 0))
                pltpu.make_async_remote_copy(
                    src_ref=kv.at[i, n, tail, :],
                    dst_ref=kv.at[i, n, tail, :],
                    send_sem=z_send.at[i, n, 0],
                    recv_sem=kv_recv.at[i, n, c],
                    device_id={"section": partner},
                    device_id_type=MESH,
                ).wait_recv()

    def w_part(n, c, owner):
        return w_hbm.at[
            pl.ds((c * heads + n) * HEAD_DIM, HEAD_DIM),
            pl.ds(pl.multiple_of(owner * features, features), features),
        ]

    def w_local(n, c):
        return pltpu.make_async_copy(
            w_part(n, c, section),
            wbuf.at[mixed(0, n, c), :],
            w_own.at[n, c],
        )

    def w_copy(n, c):
        return pltpu.make_async_remote_copy(
            src_ref=w_part(n, c, partner),
            dst_ref=wbuf.at[mixed(1, n, c), :],
            send_sem=w_send.at[n, c],
            recv_sem=w_recv.at[n, c],
            device_id={"section": partner},
            device_id_type=MESH,
        )

    def mix_copy(n, first, extent):
        return pltpu.make_async_remote_copy(
            src_ref=amix.at[:, mixed(0, n, first, extent)],
            dst_ref=amix.at[:, mixed(1, n, first, extent)],
            send_sem=mix_send.at[n, first],
            recv_sem=mix_recv.at[n, first],
            device_id={"section": partner},
            device_id_type=MESH,
        )

    h_load = pltpu.make_async_copy(h_hbm, hbuf, h_sem.at[0])
    pat_load = pltpu.make_async_copy(pattern_hbm, patterns.at[role], pat_own.at[0])

    barrier = pltpu.get_barrier_semaphore()
    for e in range(1, GROUP - 1):
        pl.semaphore_signal(barrier, inc=1, device_id=to_peer(peers[e]), device_id_type=MESH)
    pl.semaphore_signal(barrier, inc=1, device_id={"section": partner}, device_id_type=MESH)

    @pl.when(has_prev)
    def _():
        pl.semaphore_signal(
            barrier, inc=1, device_id={"seq": shard - GROUP}, device_id_type=MESH
        )

    @pl.when(has_next)
    def _():
        pl.semaphore_signal(
            barrier, inc=1, device_id={"seq": shard + GROUP}, device_id_type=MESH
        )

    pat_load.start()
    for n in range(heads):
        for i in range(2):
            kv_local(i, n).start()
        q_local(n).start()

    pl.semaphore_wait(
        barrier, GROUP - 1 + has_prev.astype(jnp.int32) + has_next.astype(jnp.int32)
    )

    pl.semaphore_signal(entered, inc=1, device_id=to_peer(peers[1]), device_id_type=MESH)

    def send(kind, n, e):
        if kind == 2:
            q_copy(n, e).start()
        else:
            kv_copy(kind, n, e).start()

    for e in (1, 2):
        pat_copy(e).start()
        send(0, 0, e)
    z_start(0, 0, role, True)
    z_start(1, 0, role, True)
    pl.semaphore_wait(entered, 1)
    pat_copy(0).start()
    send(0, 0, 0)
    for n in range(heads):
        for kind in range(3):
            if n + kind > 0:
                for e in range(GROUP - 1):
                    send(kind, n, e)
                if n == 1 and kind < 2:
                    z_start(kind, n, role, True)
        if n == 0:
            @pl.when(role == 0)
            def _():
                for m in range(2, heads):
                    for i in range(2):
                        z_start(i, m, role, True)

    for n in range(heads):
        for c in range(GROUP):
            w_copy(n, c).start()
            w_local(n, c).start()
    h_load.start()

    @pl.when(jnp.logical_not(has_prev))
    def _():
        for n in range(heads):
            kv[:, n, 0 : GROUP * rows, :] = jnp.zeros((2, GROUP * rows, HEAD_DIM), kv.dtype)

    pat_load.wait()
    for e in range(GROUP - 1):
        pat_arrive(peers[e])

    query_place = lax.broadcasted_iota(jnp.int32, (BLOCK, BLOCK), 0)
    key_place = lax.broadcasted_iota(jnp.int32, (BLOCK, BLOCK), 1)
    span_blocks = span // BLOCK
    for c in range(GROUP):
        for i in range(blocks):
            for g in range(span_blocks):
                j = i + WINDOW_BLOCKS - 1 - g
                if j < 0 or j >= WINDOW_BLOCKS:
                    value = jnp.full((BLOCK, BLOCK), HIDE, jnp.float32)
                else:
                    valid = (first_shard + c) * blocks + i - j >= 0
                    floor = jnp.where(valid, 0.0, HIDE).astype(jnp.float32)
                    level = jnp.where(patterns[c, i : i + 1, j : j + 1] == 1, floor, HIDE)
                    value = jnp.broadcast_to(level, (BLOCK, BLOCK))
                    if j == 0:
                        value = jnp.where(key_place <= query_place, value, HIDE)
                bias[c, i * BLOCK : (i + 1) * BLOCK, g * BLOCK : (g + 1) * BLOCK] = value

    factor = math.log2(math.e) / math.sqrt(HEAD_DIM)
    tile = math.gcd(features, 512)

    def forward(n):
        for i in range(2):
            for e in (1, 2, 0):
                kv_arrive(i, n, GROUP + peers[e])
                z_start(i, n, peers[e], False)
        for i in range(2):
            kv_local(i, n).wait()

        @pl.when((n + 2 < heads) & (role > 0))
        def _():
            for i in range(2):
                z_start(i, jnp.minimum(n + 2, heads - 1), role, True)

    def attend(n, c):
        keys_at = pl.ds(pl.multiple_of(c * rows + skip, BLOCK), span)
        scores = lax.dot_general(
            qbuf[n, place(c), :], kv[0, n, keys_at, :], (((1,), (1,)), ((), ())),
            preferred_element_type=jnp.float32,
        )
        scores = scores * factor + bias[c]
        largest = jnp.max(scores, axis=1, keepdims=True)
        exponent = jnp.exp2(scores - largest)
        total = jnp.sum(exponent, axis=1, keepdims=True)
        mixture = jnp.dot(
            exponent.astype(jnp.bfloat16), kv[1, n, keys_at, :],
            preferred_element_type=jnp.float32,
        )
        return (mixture * (1.0 / total)).astype(jnp.bfloat16)

    def units(n, chosen):
        for e in chosen:
            if e is None:
                q_local(n).wait()
            else:
                q_arrive(n, peers[e])
        results = [attend(n, role if e is None else peers[e]) for e in chosen]
        for e, result in zip(chosen, results):
            if e is None:
                amix[:, mixed(0, n, role)] = result
            else:
                obuf[n, place(peers[e]), :] = result
        for e in chosen:
            if e is not None:
                o_copy(n, peers[e]).start()

    chunk_depth = GROUP * HEAD_DIM
    last = heads - 1
    hold = max(last - 1, 1)

    def product(block, extent, t):
        depth = slice(block * chunk_depth, (block + extent) * chunk_depth)
        return jnp.dot(
            amix[:, depth], wbuf[depth, t : t + tile], preferred_element_type=jnp.float32
        )

    def project(block, extent, first=False):
        for t in range(0, features, tile):
            if first:
                acc[:, t : t + tile] = hbuf[:, t : t + tile].astype(jnp.float32) + product(
                    block, extent, t
                )
            else:
                acc[:, t : t + tile] += product(block, extent, t)

    def own_ready(n):
        for e in range(GROUP - 1):
            o_arrive(n, peers[e])
        mix_copy(n, 0, GROUP).start()
        for c in range(GROUP):
            w_local(n, c).wait()

    def other_ready(n):
        for c in range(GROUP):
            w_copy(n, c).wait_recv()
        mix_copy(n, 0, GROUP).wait_recv()

    def chunk(n):
        for c in reversed(range(GROUP)):
            z_arrive(n, c)
        for e in (0, 1, 2, None):
            units(n, (e,))

    @pl.loop(0, heads)
    def _(n):
        forward(n)

        @pl.when(n >= 1)
        def _():
            chunk(n - 1)

    for n in range(last):
        if n == max(last - 2, 0):
            chunk(last)
            mix_copy(last, role, 1).start()
        own_ready(n)
        if n == 0:
            h_load.wait()
            project(0, 1, True)
        else:
            other_ready(n - 1)
            project(2 * n - 1, 2)
    for c in range(GROUP):
        w_local(last, c).wait()
        w_copy(last, c).wait_recv()
    for e in range(GROUP - 1):
        o_arrive(last, peers[e])
        mix_copy(last, peers[e], 1).start()
    other_ready(last - 1)
    project(2 * last - 1, 2)
    for c in range(GROUP):
        mix_copy(last, c, 1).wait_recv()
    lanes = jnp.zeros(square_out.shape, jnp.float32)
    for t in range(0, features, tile):
        stream = acc[:, t : t + tile] + product(2 * last + 1, 1, t)
        stream_ref[:, t : t + tile] = stream
        squares = stream * stream
        for p in range(0, tile, 128):
            lanes = lanes + squares[:, p : p + 128]
    square_out[...] = lanes

    square_copy = pltpu.make_async_remote_copy(
        src_ref=square_out,
        dst_ref=square_in,
        send_sem=sq_sem.at[0],
        recv_sem=sq_sem.at[1],
        device_id={"section": partner},
        device_id_type=MESH,
    )
    square_copy.start()

    for e in range(GROUP - 1):
        pat_copy(e).wait_send()

    @pl.loop(0, heads)
    def _(n):
        for e in range(GROUP - 1):
            for i in range(2):
                kv_copy(i, n, e).wait_send()
            q_copy(n, e).wait_send()
            o_copy(n, peers[e]).wait_send()
        for i in range(2):
            for c in range(GROUP):
                z_end(i, n, c)

    for n in range(heads):
        for c in range(GROUP):
            w_copy(n, c).wait_send()
            if n == last:
                mix_copy(n, c, 1).wait_send()
        if n < last:
            mix_copy(n, 0, GROUP).wait_send()
    square_copy.wait()
    square_ref[...] = square_out[...] + square_in[...]


def shards(queries, key_rows, value_rows, block_pattern, out_weight, hidden, norm_gain):
    rows, width = queries.shape
    model = out_weight.shape[1]
    heads = width // (GROUP * HEAD_DIM)
    features = hidden.shape[1]
    span = (WINDOW_BLOCKS - 1) * BLOCK + rows
    anywhere = pl.BlockSpec(memory_space=pl.ANY)
    vmem = pl.BlockSpec(memory_space=pltpu.VMEM)
    bf16 = jnp.bfloat16
    stream, squares = pl.pallas_call(
        kernel,
        out_shape=(
            jax.ShapeDtypeStruct((rows, features), jnp.float32),
            jax.ShapeDtypeStruct((rows, 128), jnp.float32),
        ),
        in_specs=[anywhere] * 6,
        out_specs=(vmem, vmem),
        scratch_shapes=[
            pltpu.VMEM((2, heads, 2 * GROUP * rows, HEAD_DIM), bf16),
            pltpu.VMEM((heads, GROUP * rows, HEAD_DIM), bf16),
            pltpu.VMEM((heads, GROUP * rows, HEAD_DIM), bf16),
            pltpu.VMEM((rows, 2 * width), bf16),
            pltpu.VMEM((2 * width, features), bf16),
            pltpu.VMEM((rows, features), bf16),
            pltpu.VMEM((GROUP,) + block_pattern.shape, jnp.int32),
            pltpu.VMEM((GROUP, rows, span), jnp.float32),
            pltpu.VMEM((rows, features), jnp.float32),
            pltpu.VMEM((rows, 128), jnp.float32),
            pltpu.VMEM((rows, 128), jnp.float32),
            pltpu.SemaphoreType.DMA((2, heads)),
            pltpu.SemaphoreType.DMA((heads,)),
            pltpu.SemaphoreType.DMA((1,)),
            pltpu.SemaphoreType.DMA((heads, GROUP)),
            pltpu.SemaphoreType.DMA((heads, GROUP)),
            pltpu.SemaphoreType.DMA((heads, GROUP)),
            pltpu.SemaphoreType.DMA((1,)),
            pltpu.SemaphoreType.DMA((2, heads, GROUP - 1)),
            pltpu.SemaphoreType.DMA((2, heads, 2 * GROUP)),
            pltpu.SemaphoreType.DMA((2, heads, GROUP)),
            pltpu.SemaphoreType.DMA((heads, GROUP - 1)),
            pltpu.SemaphoreType.DMA((heads, GROUP)),
            pltpu.SemaphoreType.DMA((heads, GROUP)),
            pltpu.SemaphoreType.DMA((heads, GROUP)),
            pltpu.SemaphoreType.DMA((GROUP - 1,)),
            pltpu.SemaphoreType.DMA((GROUP,)),
            pltpu.SemaphoreType.DMA((heads, GROUP)),
            pltpu.SemaphoreType.DMA((heads, GROUP)),
            pltpu.SemaphoreType.DMA((2,)),
            pltpu.SemaphoreType.REGULAR,
        ],
        compiler_params=pltpu.CompilerParams(
            collective_id=0, has_side_effects=True, vmem_limit_bytes=40 * 1024 * 1024
        ),
    )(
        *[
            pltpu.with_memory_space_constraint(value, pltpu.HBM)
            for value in (
                queries, key_rows, value_rows, block_pattern, out_weight, hidden
            )
        ]
    )
    mean_square = jnp.sum(squares, axis=1, keepdims=True) / model
    normed = stream * lax.rsqrt(mean_square + 1e-06) * norm_gain[None, :]
    return (stream.astype(jnp.bfloat16), normed.astype(jnp.bfloat16))


def solution(mesh):
    placed = (
        P("seq", "section"),
        P("seq", "section"),
        P("seq", "section"),
        P("seq", None),
        P("section", None),
        P("seq", "section"),
        P("section"),
    )
    return jax.shard_map(
        shards,
        mesh=mesh,
        in_specs=placed,
        out_specs=(P("seq", "section"), P("seq", "section")),
        check_vma=False,
    )
```

```python
import math

import jax
import jax.numpy as jnp
from jax import lax
from jax.experimental import pallas as pl
from jax.experimental.pallas import tpu as pltpu
from jax.sharding import PartitionSpec as P

HEAD_DIM = 128
BLOCK = 128
WINDOW_BLOCKS = 8
GROUP = 4
MESH = pl.DeviceIdType.MESH
HIDE = -1e30


def kernel(
    q_hbm, k_hbm, v_hbm, pattern_hbm, w_hbm, h_hbm,
    stream_ref, square_ref,
    kv, qbuf, obuf, amix, wbuf, hbuf, patterns, bias, acc, square_out, square_in,
    kv_own, q_own, pat_own, w_own, w_send, w_recv, h_sem,
    kv_send, kv_recv, z_send, q_send, q_recv, o_send, o_recv, pat_send, pat_recv,
    mix_send, mix_recv, sq_sem, entered,
):
    rows, width = q_hbm.shape
    features = h_hbm.shape[1]
    heads = kv.shape[1]
    blocks = rows // BLOCK
    front = (WINDOW_BLOCKS - 1) * BLOCK
    span = front + rows
    skip = GROUP * rows - front
    shard = lax.axis_index("seq")
    section = lax.axis_index("section")
    count = lax.axis_size("seq")
    role = lax.rem(shard, GROUP)
    first_shard = shard - role
    has_prev = shard >= GROUP
    has_next = shard + GROUP < count
    partner = 1 - section
    low = lax.rem(role, 2)
    high = role // 2
    peers = (3 - role, 2 * high + 1 - low, 2 * (1 - high) + low)
    sources = (k_hbm, v_hbm)

    def head_cols(home, n):
        return pl.ds(pl.multiple_of((home * heads + n) * HEAD_DIM, HEAD_DIM), HEAD_DIM)

    def place(slot):
        return pl.ds(pl.multiple_of(slot * rows, rows), rows)

    def to_peer(peer):
        return {"seq": first_shard + peer}

    def kv_local(i, n):
        return pltpu.make_async_copy(
            sources[i].at[:, head_cols(role, n)],
            kv.at[i, n, place(GROUP + role), :],
            kv_own.at[i, n],
        )

    def q_local(n):
        return pltpu.make_async_copy(
            q_hbm.at[:, head_cols(role, n)], qbuf.at[n, place(role), :], q_own.at[n]
        )

    def kv_copy(i, n, e):
        return pltpu.make_async_remote_copy(
            src_ref=sources[i].at[:, head_cols(peers[e], n)],
            dst_ref=kv.at[i, n, place(GROUP + role), :],
            send_sem=kv_send.at[i, n, e],
            recv_sem=kv_recv.at[i, n, GROUP + role],
            device_id=to_peer(peers[e]),
            device_id_type=MESH,
        )

    def kv_arrive(i, n, slot):
        pltpu.make_async_remote_copy(
            src_ref=kv.at[i, n, place(slot), :],
            dst_ref=kv.at[i, n, place(slot), :],
            send_sem=kv_send.at[i, n, 0],
            recv_sem=kv_recv.at[i, n, slot],
            device_id={"section": partner},
            device_id_type=MESH,
        ).wait_recv()

    def q_copy(n, e):
        return pltpu.make_async_remote_copy(
            src_ref=q_hbm.at[:, head_cols(peers[e], n)],
            dst_ref=qbuf.at[n, place(role), :],
            send_sem=q_send.at[n, e],
            recv_sem=q_recv.at[n, role],
            device_id=to_peer(peers[e]),
            device_id_type=MESH,
        )

    def q_arrive(n, c):
        pltpu.make_async_remote_copy(
            src_ref=qbuf.at[n, place(c), :],
            dst_ref=qbuf.at[n, place(c), :],
            send_sem=q_send.at[n, 0],
            recv_sem=q_recv.at[n, c],
            device_id={"section": partner},
            device_id_type=MESH,
        ).wait_recv()

    def mixed(k, n, c, extent=1):
        start = ((2 * n + k) * GROUP + c) * HEAD_DIM
        return pl.ds(pl.multiple_of(start, HEAD_DIM), extent * HEAD_DIM)

    def o_copy(n, c):
        return pltpu.make_async_remote_copy(
            src_ref=obuf.at[n, place(c), :],
            dst_ref=amix.at[:, mixed(0, n, role)],
            send_sem=o_send.at[n, c],
            recv_sem=o_recv.at[n, role],
            device_id=to_peer(c),
            device_id_type=MESH,
        )

    def o_arrive(n, c):
        pltpu.make_async_remote_copy(
            src_ref=amix.at[:, mixed(0, n, c)],
            dst_ref=amix.at[:, mixed(0, n, c)],
            send_sem=o_send.at[n, 0],
            recv_sem=o_recv.at[n, c],
            device_id={"section": partner},
            device_id_type=MESH,
        ).wait_recv()

    def pat_copy(e):
        return pltpu.make_async_remote_copy(
            src_ref=pattern_hbm,
            dst_ref=patterns.at[role],
            send_sem=pat_send.at[e],
            recv_sem=pat_recv.at[role],
            device_id=to_peer(peers[e]),
            device_id_type=MESH,
        )

    def pat_arrive(c):
        pltpu.make_async_remote_copy(
            src_ref=patterns.at[c],
            dst_ref=patterns.at[c],
            send_sem=pat_send.at[0],
            recv_sem=pat_recv.at[c],
            device_id={"section": partner},
            device_id_type=MESH,
        ).wait_recv()

    def z_copies(i, n, c, own):
        def one(first, extent):
            if own:
                source = sources[i].at[pl.ds(first, extent), head_cols(role, n)]
            else:
                source = kv.at[
                    i, n, pl.ds(pl.multiple_of((GROUP + c) * rows + first, BLOCK), extent), :
                ]
            return pltpu.make_async_remote_copy(
                src_ref=source,
                dst_ref=kv.at[i, n, pl.ds(pl.multiple_of(c * rows + first, BLOCK), extent), :],
                send_sem=z_send.at[i, n, c],
                recv_sem=kv_recv.at[i, n, c],
                device_id={"seq": shard + GROUP},
                device_id_type=MESH,
            )

        return one(skip, rows - skip), one(0, rows)

    def z_act(i, n, c, own, act):
        tail, full = z_copies(i, n, c, own)

        @pl.when(has_next & (c == 0))
        def _():
            act(tail)

        @pl.when(has_next & (c > 0))
        def _():
            act(full)

    def z_start(i, n, c, own):
        z_act(i, n, c, own, lambda copy: copy.start())

    def z_end(i, n, c):
        z_act(i, n, c, False, lambda copy: copy.wait_send())

    def z_arrive(n, c):
        @pl.when(has_prev)
        def _():
            for i in range(2):
                tail = pl.ds(c * rows + (skip if c == 0 else 0), rows - (skip if c == 0 else 0))
                pltpu.make_async_remote_copy(
                    src_ref=kv.at[i, n, tail, :],
                    dst_ref=kv.at[i, n, tail, :],
                    send_sem=z_send.at[i, n, 0],
                    recv_sem=kv_recv.at[i, n, c],
                    device_id={"section": partner},
                    device_id_type=MESH,
                ).wait_recv()

    def w_part(n, c, owner):
        return w_hbm.at[
            pl.ds((c * heads + n) * HEAD_DIM, HEAD_DIM),
            pl.ds(pl.multiple_of(owner * features, features), features),
        ]

    def w_local(n, c):
        return pltpu.make_async_copy(
            w_part(n, c, section),
            wbuf.at[mixed(0, n, c), :],
            w_own.at[n, c],
        )

    def w_copy(n, c):
        return pltpu.make_async_remote_copy(
            src_ref=w_part(n, c, partner),
            dst_ref=wbuf.at[mixed(1, n, c), :],
            send_sem=w_send.at[n, c],
            recv_sem=w_recv.at[n, c],
            device_id={"section": partner},
            device_id_type=MESH,
        )

    def mix_copy(n, first, extent):
        return pltpu.make_async_remote_copy(
            src_ref=amix.at[:, mixed(0, n, first, extent)],
            dst_ref=amix.at[:, mixed(1, n, first, extent)],
            send_sem=mix_send.at[n, first],
            recv_sem=mix_recv.at[n, first],
            device_id={"section": partner},
            device_id_type=MESH,
        )

    h_load = pltpu.make_async_copy(h_hbm, hbuf, h_sem.at[0])
    pat_load = pltpu.make_async_copy(pattern_hbm, patterns.at[role], pat_own.at[0])

    barrier = pltpu.get_barrier_semaphore()
    for e in range(1, GROUP - 1):
        pl.semaphore_signal(barrier, inc=1, device_id=to_peer(peers[e]), device_id_type=MESH)
    pl.semaphore_signal(barrier, inc=1, device_id={"section": partner}, device_id_type=MESH)

    @pl.when(has_prev)
    def _():
        pl.semaphore_signal(
            barrier, inc=1, device_id={"seq": shard - GROUP}, device_id_type=MESH
        )

    @pl.when(has_next)
    def _():
        pl.semaphore_signal(
            barrier, inc=1, device_id={"seq": shard + GROUP}, device_id_type=MESH
        )

    pat_load.start()
    for n in range(heads):
        for i in range(2):
            kv_local(i, n).start()
        q_local(n).start()

    pl.semaphore_wait(
        barrier, GROUP - 1 + has_prev.astype(jnp.int32) + has_next.astype(jnp.int32)
    )

    pl.semaphore_signal(entered, inc=1, device_id=to_peer(peers[1]), device_id_type=MESH)

    def send(kind, n, e):
        if kind == 2:
            q_copy(n, e).start()
        else:
            kv_copy(kind, n, e).start()

    for e in (1, 2):
        send(0, 0, e)
        pat_copy(e).start()
    z_start(0, 0, role, True)
    z_start(1, 0, role, True)
    pl.semaphore_wait(entered, 1)
    send(0, 0, 0)
    pat_copy(0).start()
    for n in range(heads):
        for kind in range(3):
            if n + kind > 0:
                for e in range(GROUP - 1):
                    send(kind, n, e)
                if n == 1 and kind < 2:
                    z_start(kind, n, role, True)
        if n == 0:
            @pl.when(role == 0)
            def _():
                for m in range(2, heads):
                    for i in range(2):
                        z_start(i, m, role, True)

    for n in range(heads):
        for c in range(GROUP):
            w_copy(n, c).start()
            w_local(n, c).start()
    h_load.start()

    @pl.when(jnp.logical_not(has_prev))
    def _():
        for n in range(heads):
            kv[:, n, 0 : GROUP * rows, :] = jnp.zeros((2, GROUP * rows, HEAD_DIM), kv.dtype)

    pat_load.wait()
    for e in range(GROUP - 1):
        pat_arrive(peers[e])

    query_place = lax.broadcasted_iota(jnp.int32, (BLOCK, BLOCK), 0)
    key_place = lax.broadcasted_iota(jnp.int32, (BLOCK, BLOCK), 1)
    span_blocks = span // BLOCK
    for c in range(GROUP):
        for i in range(blocks):
            for g in range(span_blocks):
                j = i + WINDOW_BLOCKS - 1 - g
                if j < 0 or j >= WINDOW_BLOCKS:
                    value = jnp.full((BLOCK, BLOCK), HIDE, jnp.float32)
                else:
                    valid = (first_shard + c) * blocks + i - j >= 0
                    floor = jnp.where(valid, 0.0, HIDE).astype(jnp.float32)
                    level = jnp.where(patterns[c, i : i + 1, j : j + 1] == 1, floor, HIDE)
                    value = jnp.broadcast_to(level, (BLOCK, BLOCK))
                    if j == 0:
                        value = jnp.where(key_place <= query_place, value, HIDE)
                bias[c, i * BLOCK : (i + 1) * BLOCK, g * BLOCK : (g + 1) * BLOCK] = value

    factor = math.log2(math.e) / math.sqrt(HEAD_DIM)
    tile = math.gcd(features, 512)

    def forward(n):
        for i in range(2):
            for e in (1, 2, 0):
                kv_arrive(i, n, GROUP + peers[e])
                z_start(i, n, peers[e], False)
        for i in range(2):
            kv_local(i, n).wait()

        @pl.when((n + 2 < heads) & (role > 0))
        def _():
            for i in range(2):
                z_start(i, jnp.minimum(n + 2, heads - 1), role, True)

    def attend(n, c):
        keys_at = pl.ds(pl.multiple_of(c * rows + skip, BLOCK), span)
        scores = lax.dot_general(
            qbuf[n, place(c), :], kv[0, n, keys_at, :], (((1,), (1,)), ((), ())),
            preferred_element_type=jnp.float32,
        )
        scores = scores * factor + bias[c]
        largest = jnp.max(scores, axis=1, keepdims=True)
        exponent = jnp.exp2(scores - largest)
        total = jnp.sum(exponent, axis=1, keepdims=True)
        mixture = jnp.dot(
            exponent.astype(jnp.bfloat16), kv[1, n, keys_at, :],
            preferred_element_type=jnp.float32,
        )
        return (mixture * (1.0 / total)).astype(jnp.bfloat16)

    def units(n, chosen):
        for e in chosen:
            if e is None:
                q_local(n).wait()
            else:
                q_arrive(n, peers[e])
        results = [attend(n, role if e is None else peers[e]) for e in chosen]
        for e, result in zip(chosen, results):
            if e is None:
                amix[:, mixed(0, n, role)] = result
            else:
                obuf[n, place(peers[e]), :] = result
        for e in chosen:
            if e is not None:
                o_copy(n, peers[e]).start()

    chunk_depth = GROUP * HEAD_DIM
    last = heads - 1
    hold = max(last - 1, 1)

    def product(block, extent, t):
        depth = slice(block * chunk_depth, (block + extent) * chunk_depth)
        return jnp.dot(
            amix[:, depth], wbuf[depth, t : t + tile], preferred_element_type=jnp.float32
        )

    def project(block, extent, first=False):
        for t in range(0, features, tile):
            if first:
                acc[:, t : t + tile] = hbuf[:, t : t + tile].astype(jnp.float32) + product(
                    block, extent, t
                )
            else:
                acc[:, t : t + tile] += product(block, extent, t)

    def own_ready(n):
        for e in range(GROUP - 1):
            o_arrive(n, peers[e])
        mix_copy(n, 0, GROUP).start()
        for c in range(GROUP):
            w_local(n, c).wait()

    def other_ready(n):
        for c in range(GROUP):
            w_copy(n, c).wait_recv()
        mix_copy(n, 0, GROUP).wait_recv()

    def chunk(n):
        for c in reversed(range(GROUP)):
            z_arrive(n, c)
        for e in (0, 1, 2, None):
            units(n, (e,))

    @pl.loop(0, heads)
    def _(n):
        forward(n)

        @pl.when(n >= 1)
        def _():
            chunk(n - 1)

    for n in range(last):
        if n == max(last - 2, 0):
            chunk(last)
            mix_copy(last, role, 1).start()
        own_ready(n)
        if n == 0:
            h_load.wait()
            project(0, 1, True)
        else:
            other_ready(n - 1)
            project(2 * n - 1, 2)
    for c in range(GROUP):
        w_local(last, c).wait()
        w_copy(last, c).wait_recv()
    for e in range(GROUP - 1):
        o_arrive(last, peers[e])
        mix_copy(last, peers[e], 1).start()
    other_ready(last - 1)
    project(2 * last - 1, 2)
    for c in range(GROUP):
        mix_copy(last, c, 1).wait_recv()
    lanes = jnp.zeros(square_out.shape, jnp.float32)
    for t in range(0, features, tile):
        stream = acc[:, t : t + tile] + product(2 * last + 1, 1, t)
        stream_ref[:, t : t + tile] = stream
        squares = stream * stream
        for p in range(0, tile, 128):
            lanes = lanes + squares[:, p : p + 128]
    square_out[...] = lanes

    square_copy = pltpu.make_async_remote_copy(
        src_ref=square_out,
        dst_ref=square_in,
        send_sem=sq_sem.at[0],
        recv_sem=sq_sem.at[1],
        device_id={"section": partner},
        device_id_type=MESH,
    )
    square_copy.start()

    for e in range(GROUP - 1):
        pat_copy(e).wait_send()

    @pl.loop(0, heads)
    def _(n):
        for e in range(GROUP - 1):
            for i in range(2):
                kv_copy(i, n, e).wait_send()
            q_copy(n, e).wait_send()
            o_copy(n, peers[e]).wait_send()
        for i in range(2):
            for c in range(GROUP):
                z_end(i, n, c)

    for n in range(heads):
        for c in range(GROUP):
            w_copy(n, c).wait_send()
            if n == last:
                mix_copy(n, c, 1).wait_send()
        if n < last:
            mix_copy(n, 0, GROUP).wait_send()
    square_copy.wait()
    square_ref[...] = square_out[...] + square_in[...]


def shards(queries, key_rows, value_rows, block_pattern, out_weight, hidden, norm_gain):
    rows, width = queries.shape
    model = out_weight.shape[1]
    heads = width // (GROUP * HEAD_DIM)
    features = hidden.shape[1]
    span = (WINDOW_BLOCKS - 1) * BLOCK + rows
    anywhere = pl.BlockSpec(memory_space=pl.ANY)
    vmem = pl.BlockSpec(memory_space=pltpu.VMEM)
    bf16 = jnp.bfloat16
    stream, squares = pl.pallas_call(
        kernel,
        out_shape=(
            jax.ShapeDtypeStruct((rows, features), jnp.float32),
            jax.ShapeDtypeStruct((rows, 128), jnp.float32),
        ),
        in_specs=[anywhere] * 6,
        out_specs=(vmem, vmem),
        scratch_shapes=[
            pltpu.VMEM((2, heads, 2 * GROUP * rows, HEAD_DIM), bf16),
            pltpu.VMEM((heads, GROUP * rows, HEAD_DIM), bf16),
            pltpu.VMEM((heads, GROUP * rows, HEAD_DIM), bf16),
            pltpu.VMEM((rows, 2 * width), bf16),
            pltpu.VMEM((2 * width, features), bf16),
            pltpu.VMEM((rows, features), bf16),
            pltpu.VMEM((GROUP,) + block_pattern.shape, jnp.int32),
            pltpu.VMEM((GROUP, rows, span), jnp.float32),
            pltpu.VMEM((rows, features), jnp.float32),
            pltpu.VMEM((rows, 128), jnp.float32),
            pltpu.VMEM((rows, 128), jnp.float32),
            pltpu.SemaphoreType.DMA((2, heads)),
            pltpu.SemaphoreType.DMA((heads,)),
            pltpu.SemaphoreType.DMA((1,)),
            pltpu.SemaphoreType.DMA((heads, GROUP)),
            pltpu.SemaphoreType.DMA((heads, GROUP)),
            pltpu.SemaphoreType.DMA((heads, GROUP)),
            pltpu.SemaphoreType.DMA((1,)),
            pltpu.SemaphoreType.DMA((2, heads, GROUP - 1)),
            pltpu.SemaphoreType.DMA((2, heads, 2 * GROUP)),
            pltpu.SemaphoreType.DMA((2, heads, GROUP)),
            pltpu.SemaphoreType.DMA((heads, GROUP - 1)),
            pltpu.SemaphoreType.DMA((heads, GROUP)),
            pltpu.SemaphoreType.DMA((heads, GROUP)),
            pltpu.SemaphoreType.DMA((heads, GROUP)),
            pltpu.SemaphoreType.DMA((GROUP - 1,)),
            pltpu.SemaphoreType.DMA((GROUP,)),
            pltpu.SemaphoreType.DMA((heads, GROUP)),
            pltpu.SemaphoreType.DMA((heads, GROUP)),
            pltpu.SemaphoreType.DMA((2,)),
            pltpu.SemaphoreType.REGULAR,
        ],
        compiler_params=pltpu.CompilerParams(
            collective_id=0, has_side_effects=True, vmem_limit_bytes=40 * 1024 * 1024
        ),
    )(
        *[
            pltpu.with_memory_space_constraint(value, pltpu.HBM)
            for value in (
                queries, key_rows, value_rows, block_pattern, out_weight, hidden
            )
        ]
    )
    mean_square = jnp.sum(squares, axis=1, keepdims=True) / model
    normed = stream * lax.rsqrt(mean_square + 1e-06) * norm_gain[None, :]
    return (stream.astype(jnp.bfloat16), normed.astype(jnp.bfloat16))


def solution(mesh):
    placed = (
        P("seq", "section"),
        P("seq", "section"),
        P("seq", "section"),
        P("seq", None),
        P("section", None),
        P("seq", "section"),
        P("section"),
    )
    return jax.shard_map(
        shards,
        mesh=mesh,
        in_specs=placed,
        out_specs=(P("seq", "section"), P("seq", "section")),
        check_vma=False,
    )
```
